512 devices in a mesh: rows: 64 (over x, y, core), vec: 8 (over z).
Axes of the slice: x: 4, y: 8, z: 8, core: 2. Of those that a mesh axis runs over, the one named last changes fastest.
Arguments:
- vectors: float32 [64, 131072], P('vec', 'rows'), may hold values from -6 to 6
- damage: float32 [131072], P('rows')
- diag_blocks: bfloat16 [1024, 128, 128], P('rows')
- upper_blocks: bfloat16 [8192, 128, 128], P('rows'), may hold values from -0.5 to 0.5
- block_rows: int32 [8192], P('rows'), may hold values from 0 to 1023, as said below
- block_cols: int32 [8192], P('rows'), may hold values from 1 to 1023, as said below
- live_slots: int32 [64], P('rows'), may hold values from 64 to 128, as said below
Outputs:
- product: float32 [64, 131072], P('vec', 'rows')
- projected: float32 [64, 64], P('vec')
The draws below stay inside these ranges and needn't reach their ends.
Inputs may be any that keep to these rules, and one draw needn't show every extreme that they name: `block_rows`: the slots of device d name block rows d * 16 to (d + 1) * 16 - 1; a slot whose column lies on another device names one of the last 6 of these. block_cols[s] is greater than block_rows[s], and block_cols[s] // 16 lies between d and d + 3 for a slot of device d; some slots reach d + 3. A column on device e other than d is one of the first 6 block rows of e. A pair may appear in several slots; their blocks add. `live_slots`: some device has all its slots stored.
All inputs are finite; a program needn't handle non-finite values.
Results may differ from the reference program's by a relative error of at most 0.0029.
Values may be sent and summed in bfloat16 or wider, within the bound.
No kernel may reach another device: no remote copies, remote signals or barrier semaphores. Data moves between devices by JAX's collectives and lax.ppermute only.
A program may use at most 64 MiB of HBM per device.

```python
import jax
import jax.numpy as jnp
from jax import lax

BS = 128
NV = 64
RB_DEV = 16
SLOT_DEV = 128
REACH = 4
RIM = 6
OWNERS = 64
NBLK = 1024
NDOF = 131072
SLOTS = 8192


def pattern_pair(key):
    owner = jnp.arange(SLOTS) // SLOT_DEV
    coin = jax.random.randint(jax.random.fold_in(key, 10), (SLOTS,), 0, 2)
    reach = jax.random.randint(jax.random.fold_in(key, 11), (SLOTS,), 1, REACH)
    reach = jnp.where(coin == 0, 0, reach)
    reach = jnp.minimum(reach, OWNERS - 1 - owner)
    first = jax.random.randint(jax.random.fold_in(key, 12), (SLOTS,), 0, RB_DEV)
    second = jax.random.randint(jax.random.fold_in(key, 13), (SLOTS,), 0, RB_DEV - 1)
    second = jnp.where(second >= first, second + 1, second)
    near_row = RB_DEV - RIM + jax.random.randint(jax.random.fold_in(key, 14), (SLOTS,), 0, RIM)
    near_col = jax.random.randint(jax.random.fold_in(key, 15), (SLOTS,), 0, RIM)
    row_local = jnp.where(reach == 0, jnp.minimum(first, second), near_row)
    col_local = jnp.where(reach == 0, jnp.maximum(first, second), near_col)
    rows_out = owner * RB_DEV + row_local
    cols_out = (owner + reach) * RB_DEV + col_local
    return (rows_out.astype(jnp.int32), cols_out.astype(jnp.int32))


def draw_block_rows(key, part):
    return pattern_pair(key)[0]


def draw_block_cols(key, part):
    return pattern_pair(key)[1]


def draw_live_slots(key, part):
    counts = jax.random.randint(jax.random.fold_in(key, 21), (OWNERS,), SLOT_DEV // 2, SLOT_DEV + 1)
    fullest = jax.random.randint(jax.random.fold_in(key, 22), (), 0, OWNERS)
    counts = jnp.where(jnp.arange(OWNERS) == fullest, SLOT_DEV, counts)
    return counts.astype(jnp.int32)


def draw_damage(key, part):
    base = jax.random.uniform(jax.random.fold_in(key, 31), (NDOF,), jnp.float32)
    ramp = 0.2 + 0.75 * jnp.arange(NDOF).astype(jnp.float32) / (NDOF - 1)
    return (base * ramp).astype(jnp.float32)


def draw_diag_blocks(key, part):
    noise = jax.random.normal(jax.random.fold_in(key, 41), (NBLK, BS, BS), jnp.float32)
    sym = 0.5 * (noise + jnp.swapaxes(noise, 1, 2)) / jnp.sqrt(jnp.float32(BS))
    sym = sym + 2.0 * jnp.eye(BS, dtype=jnp.float32)[None, :, :]
    return sym.astype(jnp.bfloat16)


def steps_of(stream_key, extent, pieces, low, largest):
    def one(position, parts):
        draws = jax.random.uniform(jax.random.fold_in(jax.random.fold_in(stream_key, 6), position), (parts,), jnp.float32, low / len(pieces), largest / len(pieces))
        return jnp.repeat(jnp.exp(draws), extent[position] // parts).reshape((-1,) + (1,) * (len(extent) - position - 1))

    gain = one(*pieces[0])
    for cut in pieces[1:]:
        gain = gain * one(*cut)
    return gain


def scatter_about(rng, extent, spread, most, cuts=(), kind=jnp.bfloat16):
    result = jax.random.normal(rng, extent, jnp.float32) * spread
    if len(cuts) > 0:
        result = steps_of(rng, extent, cuts, -0.22, 0.18) * result
    return jnp.clip(result, min=-most, max=most).astype(kind)


def setup_inputs(seed: int = 0) -> dict:
    arg_keys = jax.random.split(jax.random.key(seed), 8)
    return {
        "vectors": scatter_about(arg_keys[0], (NV, NDOF), 1.0, 6.0, ((0, 8), (1, 64)), jnp.float32),
        "damage": draw_damage(jax.random.fold_in(arg_keys[7], 71), 0),
        "diag_blocks": draw_diag_blocks(jax.random.fold_in(arg_keys[7], 71), 0),
        "upper_blocks": scatter_about(arg_keys[3], (SLOTS, BS, BS), BS ** -0.5, 0.5, ((0, 64),)),
        "block_rows": draw_block_rows(jax.random.fold_in(arg_keys[7], 71), 0),
        "block_cols": draw_block_cols(jax.random.fold_in(arg_keys[7], 71), 0),
        "live_slots": draw_live_slots(jax.random.fold_in(arg_keys[7], 71), 0),
    }


resid_eta = 0.001

def reference(vectors, damage, diag_blocks, upper_blocks, block_rows, block_cols, live_slots):
    soft = jnp.sqrt((1.0 - damage) ** 2 + resid_eta)
    scaled = (vectors * soft[None, :]).astype(jnp.bfloat16)
    wide = scaled.astype(jnp.float32).reshape(NV, NBLK, BS)
    accum = jnp.einsum('vrj,rij->vri', wide, diag_blocks.astype(jnp.float32), precision=lax.Precision.HIGHEST)

    def sweep(acc, block_set):
        blocks, rows_here, cols_here, live = block_set
        stored = jnp.arange(SLOT_DEV).astype(jnp.int32) < live
        dense = jnp.where(stored[:, None, None], blocks.astype(jnp.float32), jnp.zeros((), jnp.float32))
        forward = jnp.einsum('vsj,sij->vsi', wide[:, cols_here], dense, precision=lax.Precision.HIGHEST)
        backward = jnp.einsum('vsi,sij->vsj', wide[:, rows_here], dense, precision=lax.Precision.HIGHEST)
        acc = acc.at[:, rows_here].add(forward)
        acc = acc.at[:, cols_here].add(backward)
        return (acc, None)
    block_set = (upper_blocks.reshape(OWNERS, SLOT_DEV, BS, BS), block_rows.reshape(OWNERS, SLOT_DEV).astype(jnp.int32), block_cols.reshape(OWNERS, SLOT_DEV).astype(jnp.int32), live_slots.astype(jnp.int32))
    accum, unused = lax.scan(sweep, accum, block_set)
    product = soft[None, :] * accum.reshape(NV, NDOF)
    projected = jnp.dot(vectors, product.T, precision=lax.Precision.HIGHEST, preferred_element_type=jnp.float32) / NDOF
    return (product, projected)
```

```python
import jax
import jax.numpy as jnp
from jax import lax
from jax.sharding import PartitionSpec as P

REACH = 4
RIM = 6


resid_eta = 0.001


def passed_along(array, axis, by):
    devices = lax.axis_size(axis)
    pairs = [(i, i + by) for i in range(devices) if 0 <= i + by < devices]
    return lax.ppermute(array, axis, pairs)


def everyones(array, axis):
    copies = jnp.broadcast_to(array[None], (lax.axis_size(axis),) + array.shape)
    return lax.all_to_all(copies, axis, 0, 0)


def on_device(vectors, damage, diag_blocks, upper_blocks, block_rows, block_cols, live_slots):
    vec_here, width = vectors.shape
    rb_here = diag_blocks.shape[0]
    block_size = diag_blocks.shape[1]
    slot_count = upper_blocks.shape[0]
    mine = lax.axis_index("rows")
    soft = jnp.sqrt((1.0 - damage) ** 2 + resid_eta)
    flat = (vectors * soft[None, :]).astype(jnp.bfloat16)
    scaled = flat.reshape(vec_here, rb_here, block_size)
    stored = (jnp.arange(slot_count) < live_slots[0]).astype(jnp.float32)
    local_rows = block_rows - mine * rb_here
    row_pick = (local_rows[:, None] == jnp.arange(rb_here)[None, :]).astype(jnp.float32) * stored[
        :, None
    ]
    own_rows = jnp.einsum(
        "vrb,sr->vsb", scaled, row_pick.astype(jnp.bfloat16), preferred_element_type=jnp.float32
    ).astype(jnp.bfloat16)
    accum = jnp.einsum("vrj,rij->vri", scaled, diag_blocks, preferred_element_type=jnp.float32)
    backward = jnp.einsum(
        "vsi,sij->vsj", own_rows, upper_blocks, preferred_element_type=jnp.float32
    )
    pieces = [scaled]
    for step in range(1, REACH):
        pieces.append(passed_along(scaled[:, :RIM], "rows", -step))
    window = jnp.concatenate(pieces, axis=1)
    relative = block_cols - mine * rb_here
    dev_step = relative // rb_here
    within = relative - dev_step * rb_here
    col_index = jnp.where(dev_step == 0, within, rb_here + (dev_step - 1) * RIM + within)
    span = window.shape[1]
    col_pick = (col_index[:, None] == jnp.arange(span)[None, :]).astype(jnp.float32) * stored[
        :, None
    ]
    far_cols = jnp.einsum(
        "vcb,sc->vsb", window, col_pick.astype(jnp.bfloat16), preferred_element_type=jnp.float32
    ).astype(jnp.bfloat16)
    forward = jnp.einsum("vsj,sij->vsi", far_cols, upper_blocks, preferred_element_type=jnp.float32)
    gathered = jnp.einsum("vsi,sr->vri", forward, row_pick, precision=lax.Precision.HIGHEST)
    spread = jnp.einsum("vsj,sc->vcj", backward, col_pick, precision=lax.Precision.HIGHEST)
    accum = accum + gathered + spread[:, :rb_here]
    for step in range(1, REACH):
        low = rb_here + (step - 1) * RIM
        arrived = passed_along(spread[:, low : low + RIM], "rows", step)
        accum = accum.at[:, :RIM].add(arrived)
    raw = accum.reshape(vec_here, width)
    product = soft[None, :] * raw
    every = everyones(flat, "vec").reshape(-1, width)
    partial_gram = jnp.dot(
        raw,
        every.astype(jnp.float32).T,
        precision=lax.Precision.HIGHEST,
        preferred_element_type=jnp.float32,
    )
    half = vec_here // 2
    packed = jnp.concatenate([partial_gram[:half], partial_gram[half:]], axis=1)
    total_dof = width * lax.axis_size("rows")
    packed = jnp.sum(everyones(packed, "rows"), axis=0) / total_dof
    columns = partial_gram.shape[1]
    projected = jnp.concatenate([packed[:, :columns], packed[:, columns:]], axis=0)
    return (product, projected)


def solution(mesh):
    return jax.shard_map(
        on_device,
        mesh=mesh,
        in_specs=(
            P("vec", "rows"),
            P("rows"),
            P("rows", None, None),
            P("rows", None, None),
            P("rows"),
            P("rows"),
            P("rows"),
        ),
        out_specs=(P("vec", "rows"), P("vec", None)),
        check_vma=False,
    )
```

```python
import functools

import jax
import jax.numpy as jnp
from jax import lax
from jax.experimental import pallas as pl
from jax.experimental.pallas import tpu as pltpu
from jax.sharding import PartitionSpec as P

REACH = 4
RIM = 6
UNROLL = 64
VMEM_BYTES = 8 << 20
WIDE_VMEM_BYTES = 46 << 20
CHUNKS = 8


resid_eta = 0.001

VM = pl.BlockSpec(memory_space=pltpu.VMEM)
FAR = pl.BlockSpec(memory_space=pl.ANY)
SM = pl.BlockSpec(memory_space=pltpu.SMEM)
TRANSPOSED = (((1,), (1,)), ((), ()))


def passed_along(array, axis, by):
    devices = lax.axis_size(axis)
    pairs = [(i, i + by) for i in range(devices) if 0 <= i + by < devices]
    return lax.ppermute(array, axis, pairs)


def call(kernel, name, in_specs, outs, scratch, flops, moved, vmem=VMEM_BYTES):
    return pl.pallas_call(
        kernel,
        name=name,
        in_specs=in_specs,
        out_specs=[VM] * len(outs),
        out_shape=[jax.ShapeDtypeStruct(shape, dtype) for shape, dtype in outs],
        scratch_shapes=scratch,
        compiler_params=pltpu.CompilerParams(vmem_limit_bytes=vmem),
        cost_estimate=pl.CostEstimate(flops=flops, bytes_accessed=moved, transcendentals=0),
    )


def softness(damage):
    return jnp.sqrt((1.0 - damage) ** 2 + resid_eta)


def scale_kernel(vectors, damage, copies, blocks, rim):
    soft = softness(damage[...])
    size = blocks.shape[2]
    for b in range(blocks.shape[0]):
        cut = slice(b * size, (b + 1) * size)
        scaled = (vectors[:, cut] * soft[b : b + 1, :]).astype(jnp.bfloat16)
        blocks[b] = scaled
        if b < RIM:
            rim[b] = scaled
        for i in range(copies.shape[0]):
            copies[i, :, cut] = scaled


def spread_halves(upper_half, lower_half, parts, last):
    for at, ref in parts:
        for i in range(ref.shape[0]):
            x = ref[i].astype(jnp.float32)
            z = jnp.zeros_like(x)
            upper_half[at + i] = jnp.concatenate([x, z], 0).astype(jnp.bfloat16)
            lower_half[at + i] = jnp.concatenate([z, x], 0).astype(jnp.bfloat16)
    upper_half[last] = jnp.zeros(upper_half.shape[1:], jnp.bfloat16)
    lower_half[last] = jnp.zeros(lower_half.shape[1:], jnp.bfloat16)


def each_pair(start, slots, take, give, top, bottom, total, product, none_from, none_to, base, live):
    vecs = total.shape[1]

    unroll = min(slots, UNROLL)

    @pl.loop(0, slots // unroll)
    def _(group):
        first = start + group * unroll
        results = []
        for k in range(0, unroll, 2):
            s = first + k
            a = jnp.where(s < live, take[s] - base, none_from)
            b = jnp.where(s + 1 < live, take[s + 1] - base, none_from)
            x = jnp.concatenate([top[a], bottom[b]], axis=1)
            y = product(x, s)
            results += [y[:vecs], y[vecs:]]
        for k in range(unroll):
            s = first + k
            to = jnp.where(s < live, give[s] - base, none_to)
            total[to] += results[k]


def backward_kernel(
    rows, cols, place, blocks, upper_far, own, one, two, three, upper, total, top, bottom, sems
):
    here = own.shape[0]
    per = upper.shape[0] // CHUNKS

    def chunk(c):
        cut = pl.ds(c * per, per)
        return pltpu.make_async_copy(upper_far.at[cut], upper.at[cut], sems.at[c])

    for c in range(CHUNKS):
        chunk(c).start()
    total[...] = jnp.zeros_like(total)
    spread_halves(top, bottom, [(0, blocks)], here)

    def product(x, s):
        size = upper.shape[1]
        pair = upper[pl.ds(s, 2)].reshape(2 * size, size)
        return jnp.dot(x, pair, preferred_element_type=jnp.float32)

    for c in range(CHUNKS):
        chunk(c).wait()
        each_pair(
            c * per, per, rows, cols, top, bottom, total, product, here, REACH * here, place[0],
            place[1],
        )
    own[...] = total[:here]
    for step, out in ((1, one), (2, two), (3, three)):
        out[...] = total[step * here : step * here + RIM]


def forward_kernel(
    rows, cols, place, blocks, far1, far2, far3, own, back1, back2, back3, diag, every, damage,
    upper, product_out, copies, total, top, bottom
):
    here = own.shape[0]
    size = diag.shape[1]
    vecs = blocks.shape[1]
    parts = [(0, blocks), (here, far1), (2 * here, far2), (3 * here, far3)]
    spread_halves(top, bottom, parts, REACH * here)
    total[:here] = own[...]
    total[:RIM] += back1[...] + back2[...] + back3[...]

    def product(x, s):
        pair = jnp.concatenate([upper[s], upper[s + 1]], axis=1)
        return lax.dot_general(x, pair, TRANSPOSED, preferred_element_type=jnp.float32)

    each_pair(
        0, upper.shape[0], cols, rows, top, bottom, total, product, REACH * here, here, place[0],
        place[1],
    )
    soft = softness(damage[...])
    gram = jnp.zeros((2 * vecs, every.shape[0]), jnp.float32)
    for b in range(here):
        raw = total[b] + lax.dot_general(
            blocks[b], diag[b], TRANSPOSED, preferred_element_type=jnp.float32
        )
        cut = slice(b * size, (b + 1) * size)
        product_out[:, cut] = raw * soft[b : b + 1, :]
        high = raw.astype(jnp.bfloat16)
        low = (raw - high.astype(jnp.float32)).astype(jnp.bfloat16)
        gram += lax.dot_general(
            jnp.concatenate([high, low], 0), every[:, cut], TRANSPOSED,
            preferred_element_type=jnp.float32,
        )
    gram = gram[:vecs] + gram[vecs:]
    half = vecs // 2
    packed = jnp.concatenate([gram[:half], gram[half:]], axis=1)
    copies[...] = jnp.broadcast_to(packed[None], copies.shape)


def sum_kernel(scale, parts, out):
    packed = jnp.sum(parts[...], axis=0) * scale
    columns = out.shape[1]
    half = packed.shape[0]
    out[:half] = packed[:, :columns]
    out[half:] = packed[:, columns:]


def on_device(vectors, damage, diag_blocks, upper_blocks, block_rows, block_cols, live_slots):
    f32, bf16 = jnp.float32, jnp.bfloat16
    vecs, width = vectors.shape
    here, size = diag_blocks.shape[:2]
    slots = upper_blocks.shape[0]
    owners, groups = lax.axis_size("rows"), lax.axis_size("vec")
    base = lax.axis_index("rows").astype(jnp.int32) * here
    place = jnp.stack([base, live_slots[0]])
    damage = damage.reshape(here, size)
    rim = (RIM, vecs, size)

    copies, blocks, edge = call(
        scale_kernel, "scale", [VM, VM],
        [((groups, vecs, width), bf16), ((here, vecs, size), bf16), (rim, bf16)],
        [], vecs * width, 6 * vecs * width,
    )(vectors, damage)
    every = lax.all_to_all(copies, "vec", 0, 0)
    far = [passed_along(edge, "rows", -step) for step in range(1, REACH)]

    flops = 4 * slots * vecs * size * size
    moved = 2 * slots * size * size
    own, *spread, upper_near = call(
        backward_kernel, "backward", [SM, SM, SM, VM, FAR],
        [((here, vecs, size), f32)] + [(rim, f32)] * 3 + [(upper_blocks.shape, bf16)],
        [
            pltpu.VMEM((REACH * here + 1, vecs, size), f32),
            pltpu.VMEM((here + 1, 2 * vecs, size), bf16),
            pltpu.VMEM((here + 1, 2 * vecs, size), bf16),
            pltpu.SemaphoreType.DMA((CHUNKS,)),
        ],
        flops, moved, WIDE_VMEM_BYTES,
    )(block_rows, block_cols, place, blocks, upper_blocks)
    back = [passed_along(spread[step - 1], "rows", step) for step in range(1, REACH)]

    product, partials = call(
        forward_kernel, "forward", [SM] * 3 + [VM] * 12,
        [((vecs, width), f32), ((owners, vecs // 2, 2 * groups * vecs), f32)],
        [
            pltpu.VMEM((here + 1, vecs, size), f32),
            pltpu.VMEM((REACH * here + 1, 2 * vecs, size), bf16),
            pltpu.VMEM((REACH * here + 1, 2 * vecs, size), bf16),
        ],
        flops, moved,
    )(
        block_rows, block_cols, place, blocks, *far, own, *back, diag_blocks,
        every.reshape(groups * vecs, width), damage, upper_near,
    )
    partials = lax.all_to_all(partials, "rows", 0, 0)
    (projected,) = call(
        functools.partial(sum_kernel, 1.0 / (width * owners)), "sum", [VM],
        [((vecs, groups * vecs), f32)], [], 0, partials.size * 4,
    )(partials)
    return (product, projected)


def solution(mesh):
    return jax.shard_map(
        on_device,
        mesh=mesh,
        in_specs=(
            P("vec", "rows"),
            P("rows"),
            P("rows", None, None),
            P("rows", None, None),
            P("rows"),
            P("rows"),
            P("rows"),
        ),
        out_specs=(P("vec", "rows"), P("vec", None)),
        check_vma=False,
    )
```

```python
import functools

import jax
import jax.numpy as jnp
from jax import lax
from jax.experimental import pallas as pl
from jax.experimental.pallas import tpu as pltpu
from jax.sharding import PartitionSpec as P

REACH = 4
RIM = 6
PIECES = (16, 32, 32, 48)
SMALL_VMEM = 8 << 20
BLOCKS_STAY = 50 << 20
FIRST_VMEM = 53 << 20


resid_eta = 0.001

VM = pl.BlockSpec(memory_space=pltpu.VMEM)
SM = pl.BlockSpec(memory_space=pltpu.SMEM)
FAR = pl.BlockSpec(memory_space=pl.ANY)
ROW, COL, CORE = 0, 1, 2
TRANSPOSED = (((1,), (1,)), ((), ()))


def call(kernel, name, in_specs, outs, scratch, vmem, flops, moved):
    return pl.pallas_call(
        kernel,
        name=name,
        in_specs=in_specs,
        out_specs=[VM] * len(outs),
        out_shape=[jax.ShapeDtypeStruct(shape, dtype) for shape, dtype in outs],
        scratch_shapes=scratch,
        compiler_params=pltpu.CompilerParams(vmem_limit_bytes=vmem),
        cost_estimate=pl.CostEstimate(flops=flops, bytes_accessed=moved, transcendentals=0),
    )


def softness(damage):
    return jnp.sqrt((1.0 - damage) ** 2 + resid_eta)


def put_halves(top, bottom, at, x):
    z = jnp.zeros_like(x)
    top[at] = jnp.concatenate([x, z], 0).astype(jnp.bfloat16)
    bottom[at] = jnp.concatenate([z, x], 0).astype(jnp.bfloat16)


def streamed(upper_far, upper, sems):
    copies, first = [], 0
    for i, count in enumerate(PIECES):
        cut = pl.ds(first, count)
        copies.append(pltpu.make_async_copy(upper_far.at[cut], upper.at[cut], sems.at[i]))
        first += count
    assert first == upper.shape[0]
    return copies


def each_pair(first, count, where, take, give, top, bottom, total, product):
    vecs = total.shape[1]
    results = []
    for s in range(first, first + count, 2):
        x = jnp.concatenate([top[where[take, s]], bottom[where[take, s + 1]]], axis=1)
        y = product(x, s)
        results += [y[:vecs], y[vecs:]]
    for k in range(count):
        total[where[give, first + k]] += results[k]


def backward_kernel(
    where, vectors, damage, upper_far, everyones, blocks, rim, own, one, chips, swap,
    upper, total, top, bottom, sems
):
    here = own.shape[0]
    size = upper.shape[1]
    copies = streamed(upper_far, upper, sems)
    for copy in copies:
        copy.start()
    total[...] = jnp.zeros_like(total)
    soft = softness(damage[...])
    for b in range(here):
        cut = slice(b * size, (b + 1) * size)
        scaled = (vectors[:, cut] * soft[b : b + 1, :]).astype(jnp.bfloat16)
        blocks[b] = scaled
        if b < RIM:
            rim[b] = scaled
        for i in range(everyones.shape[0]):
            everyones[i, :, cut] = scaled
        put_halves(top, bottom, b, scaled.astype(jnp.float32))
    put_halves(top, bottom, here, jnp.zeros(total.shape[1:], jnp.float32))

    def product(x, s):
        pair = upper[pl.ds(s, 2)].reshape(2 * size, size)
        return jnp.dot(x, pair, preferred_element_type=jnp.float32)

    first = 0
    for copy, count in zip(copies, PIECES):
        copy.wait()
        each_pair(first, count, where, ROW, COL, top, bottom, total, product)
        first += count
    own[...] = total[:here]
    one[...] = total[here : here + RIM]
    second_core = where[CORE, 0]
    other = jnp.where(second_core == 1, here, 3 * here)
    chips[0] = total[2 * here : 2 * here + RIM]
    chips[1] = total[pl.ds(other, RIM)]
    swap[...] = jnp.where(
        second_core == 1, total[3 * here : 3 * here + RIM], blocks[:RIM].astype(jnp.float32)
    )


def relay_kernel(where, rim, far, one, chips, out):
    out[0] = rim[...].astype(jnp.float32)
    out[1] = far[...].astype(jnp.float32)
    out[2] = chips[1] + jnp.where(where[CORE, 0] == 1, 0.0, one[...])


def forward_kernel(
    where, blocks, far, chips, swap, mate, own, diag, every, damage, upper_far,
    product_out, copies_out, upper, total, top, bottom, sems
):
    here = own.shape[0]
    size = diag.shape[1]
    vecs = blocks.shape[1]
    copies = streamed(upper_far, upper, sems)
    for copy in copies:
        copy.start()
    second_core = where[CORE, 0] == 1
    for b in range(here):
        put_halves(top, bottom, b, blocks[b].astype(jnp.float32))
    for b in range(RIM):
        put_halves(top, bottom, here + b, jnp.where(second_core, mate[1, b], mate[0, b]))
        put_halves(top, bottom, 2 * here + b, far[b].astype(jnp.float32))
        put_halves(top, bottom, 3 * here + b, jnp.where(second_core, swap[b], mate[1, b]))
    put_halves(top, bottom, REACH * here, jnp.zeros((vecs, size), jnp.float32))
    for b in range(here):
        total[b] = own[b] + lax.dot_general(
            blocks[b], diag[b], TRANSPOSED, preferred_element_type=jnp.float32
        )
    total[:RIM] += chips[0] + mate[2] + jnp.where(second_core, 0.0, swap[...])

    def product(x, s):
        pair = jnp.concatenate([upper[s], upper[s + 1]], axis=1)
        return lax.dot_general(x, pair, TRANSPOSED, preferred_element_type=jnp.float32)

    first = 0
    for copy, count in zip(copies, PIECES):
        copy.wait()
        each_pair(first, count, where, COL, ROW, top, bottom, total, product)
        first += count
    soft = softness(damage[...])
    gram = jnp.zeros((2 * vecs, every.shape[0]), jnp.float32)
    for b in range(here):
        raw = total[b]
        cut = slice(b * size, (b + 1) * size)
        product_out[:, cut] = raw * soft[b : b + 1, :]
        high = raw.astype(jnp.bfloat16)
        low = (raw - high.astype(jnp.float32)).astype(jnp.bfloat16)
        gram += lax.dot_general(
            jnp.concatenate([high, low], 0), every[:, cut], TRANSPOSED,
            preferred_element_type=jnp.float32,
        )
    gram = gram[:vecs] + gram[vecs:]
    half = vecs // 2
    packed = jnp.concatenate([gram[:half], gram[half:]], axis=1)
    copies_out[...] = jnp.broadcast_to(packed[None], copies_out.shape)


def sum_kernel(scale, parts, out):
    packed = jnp.sum(parts[...], axis=0) * scale
    columns = out.shape[1]
    half = packed.shape[0]
    out[:half] = packed[:, :columns]
    out[half:] = packed[:, columns:]


def backward(groups, where, vectors, damage, upper):
    f32, bf16 = jnp.float32, jnp.bfloat16
    vecs = vectors.shape[0]
    here, size = damage.shape
    slots = upper.shape[0]
    rim = (RIM, vecs, size)
    return call(
        backward_kernel, "backward", [SM, VM, VM, FAR],
        [
            ((groups, vecs, here * size), bf16), ((here, vecs, size), bf16), (rim, bf16),
            ((here, vecs, size), f32), (rim, f32), ((2,) + rim, f32), (rim, f32),
        ],
        [
            pltpu.VMEM(upper.shape, bf16),
            pltpu.VMEM((REACH * here + 1, vecs, size), f32),
            pltpu.VMEM((here + 1, 2 * vecs, size), bf16),
            pltpu.VMEM((here + 1, 2 * vecs, size), bf16),
            pltpu.SemaphoreType.DMA((len(PIECES),)),
        ],
        FIRST_VMEM, 2 * slots * vecs * size * size, 2 * slots * size * size,
    )(where, vectors, damage, upper)


def forward(owners, where, blocks, far, chips, swap, mate, own, diag, every, damage, upper):
    f32, bf16 = jnp.float32, jnp.bfloat16
    here, vecs, size = blocks.shape
    slots = upper.shape[0]
    return call(
        forward_kernel, "forward", [SM] + [VM] * 9 + [FAR],
        [((vecs, here * size), f32), ((owners, vecs // 2, 2 * every.shape[0]), f32)],
        [
            pltpu.VMEM(upper.shape, bf16),
            pltpu.VMEM((here + 1, vecs, size), f32),
            pltpu.VMEM((REACH * here + 1, 2 * vecs, size), bf16),
            pltpu.VMEM((REACH * here + 1, 2 * vecs, size), bf16),
            pltpu.SemaphoreType.DMA((len(PIECES),)),
        ],
        BLOCKS_STAY, 2 * slots * vecs * size * size, 2 * slots * size * size,
    )(where, blocks, far, chips, swap, mate, own, diag, every, damage, upper)


def on_device(vectors, damage, diag_blocks, upper_blocks, block_rows, block_cols, live_slots):
    f32, bf16 = jnp.float32, jnp.bfloat16
    vecs, width = vectors.shape
    here, size = diag_blocks.shape[:2]
    owners, groups = lax.axis_size("rows"), lax.axis_size("vec")
    mine = lax.axis_index("rows").astype(jnp.int32)
    stored = jnp.arange(upper_blocks.shape[0]) < live_slots[0]
    rows = jnp.where(stored, block_rows - mine * here, here)
    cols = jnp.where(stored, block_cols - mine * here, REACH * here)
    where = jnp.stack([rows, cols, jnp.full_like(rows, mine & 1)])
    damage = damage.reshape(here, size)
    rim = (RIM, vecs, size)

    copies, blocks, edge, own, one, chips, swap = backward(
        groups, where, vectors, damage, upper_blocks
    )
    every = lax.all_to_all(copies, "vec", 0, 0).reshape(groups * vecs, width)

    down = [(d, d - 2) for d in range(2, owners)]
    up = [(d, d + 2) for d in range(owners - 2)]
    across = [(d, d + 3) for d in range(1, owners - 3, 2)]
    across += [(b, a) for a, b in across]
    mates = [(d, d ^ 1) for d in range(owners)]

    far = lax.ppermute(edge, "rows", down)
    chips = lax.ppermute(chips, "rows", up)
    swap = lax.ppermute(swap, "rows", across)
    (mate,) = call(
        relay_kernel, "relay", [SM] + [VM] * 4, [((3,) + rim, f32)], [], SMALL_VMEM, 0, 8 * size,
    )(where, edge, far, one, chips)
    mate = lax.ppermute(mate, "rows", mates)

    product, partials = forward(
        owners, where, blocks, far, chips, swap, mate, own, diag_blocks,
        every, damage, upper_blocks,
    )
    partials = lax.all_to_all(partials, "rows", 0, 0)
    (projected,) = call(
        functools.partial(sum_kernel, 1.0 / (width * owners)), "sum", [VM],
        [((vecs, groups * vecs), f32)], [], SMALL_VMEM, 0, partials.size * 4,
    )(partials)
    return (product, projected)


def solution(mesh):
    return jax.shard_map(
        on_device,
        mesh=mesh,
        in_specs=(
            P("vec", "rows"),
            P("rows"),
            P("rows", None, None),
            P("rows", None, None),
            P("rows"),
            P("rows"),
            P("rows"),
        ),
        out_specs=(P("vec", "rows"), P("vec", None)),
        check_vma=False,
    )
```

```python
import functools

import jax
import jax.numpy as jnp
from jax import lax
from jax.experimental import pallas as pl
from jax.experimental.pallas import tpu as pltpu
from jax.sharding import PartitionSpec as P

REACH = 4
RIM = 6
PIECES = (16, 32, 32, 48)
SMALL_VMEM = 8 << 20
BLOCKS_STAY = 16 << 20


resid_eta = 0.001

VM = pl.BlockSpec(memory_space=pltpu.VMEM)
SM = pl.BlockSpec(memory_space=pltpu.SMEM)
FAR = pl.BlockSpec(memory_space=pl.ANY)
TRANSPOSED = (((1,), (1,)), ((), ()))


def in_hbm(array):
    return pltpu.with_memory_space_constraint(array, pltpu.HBM)


def call(kernel, name, in_specs, outs, scratch, vmem, flops, moved):
    return pl.pallas_call(
        kernel,
        name=name,
        in_specs=in_specs,
        out_specs=[VM] * len(outs),
        out_shape=[jax.ShapeDtypeStruct(shape, dtype) for shape, dtype in outs],
        scratch_shapes=scratch,
        compiler_params=pltpu.CompilerParams(vmem_limit_bytes=vmem),
        cost_estimate=pl.CostEstimate(flops=flops, bytes_accessed=moved, transcendentals=0),
    )


def softness(damage):
    return jnp.sqrt((1.0 - damage) ** 2 + resid_eta)


def put_halves(top, bottom, at, x):
    z = jnp.zeros_like(x)
    top[at] = jnp.concatenate([x, z], 0).astype(jnp.bfloat16)
    bottom[at] = jnp.concatenate([z, x], 0).astype(jnp.bfloat16)


def streamed(upper_far, upper, sems):
    copies, first = [], 0
    for i, count in enumerate(PIECES):
        cut = pl.ds(first, count)
        copies.append(pltpu.make_async_copy(upper_far.at[cut], upper.at[cut], sems.at[i]))
        first += count
    assert first == upper.shape[0]
    return copies


def each_pair(first, count, live, take, give, top, bottom, total, product):
    vecs = total.shape[1]
    none_from, none_to = top.shape[0] - 1, total.shape[0] - 1

    def taken(s):
        return jnp.where(s < live, take(s), none_from)

    results = []
    for s in range(first, first + count, 2):
        y = product(jnp.concatenate([top[taken(s)], bottom[taken(s + 1)]], axis=1), s)
        results += [y[:vecs], y[vecs:]]
    for k in range(count):
        s = first + k
        total[jnp.where(s < live, give(s), none_to)] += results[k]


def backward_kernel(
    rows_far, cols_far, live_far, vectors_far, damage_far, upper_far, everyones, blocks, rim, own,
    one, chips, swap, rows, cols, live, vectors, damage, upper, total, top, bottom, sems, few_sems
):
    here = own.shape[0]
    size = upper.shape[1]
    few = [
        pltpu.make_async_copy(source, target, few_sems.at[i])
        for i, (source, target) in enumerate(
            ((vectors_far, vectors), (damage_far, damage), (rows_far, rows), (cols_far, cols),
             (live_far, live))
        )
    ]
    copies = streamed(upper_far, upper, sems)
    for copy in few + copies:
        copy.start()
    mine = lax.axis_index("rows")
    total[...] = jnp.zeros_like(total)
    for copy in few:
        copy.wait()
    soft = softness(damage[...])
    for b in range(here):
        cut = slice(b * size, (b + 1) * size)
        scaled = (vectors[:, cut] * soft[b : b + 1, :]).astype(jnp.bfloat16)
        blocks[b] = scaled
        if b < RIM:
            rim[b] = scaled
        for i in range(everyones.shape[0]):
            everyones[i, :, cut] = scaled
        put_halves(top, bottom, b, scaled.astype(jnp.float32))
    put_halves(top, bottom, here, jnp.zeros(total.shape[1:], jnp.float32))

    def product(x, s):
        pair = upper[pl.ds(s, 2)].reshape(2 * size, size)
        return jnp.dot(x, pair, preferred_element_type=jnp.float32)

    first = 0
    for copy, count in zip(copies, PIECES):
        copy.wait()
        each_pair(
            first, count, live[0], lambda s: rows[s] - mine * here, lambda s: cols[s] - mine * here,
            top, bottom, total, product,
        )
        first += count
    own[...] = total[:here]
    one[...] = total[here : here + RIM]
    second_core = lax.rem(mine, 2)
    other = jnp.where(second_core == 1, here, 3 * here)
    chips[0] = total[2 * here : 2 * here + RIM]
    chips[1] = total[pl.ds(other, RIM)]
    swap[...] = jnp.where(
        second_core == 1, total[3 * here : 3 * here + RIM], blocks[:RIM].astype(jnp.float32)
    )


def relay_kernel(rim, far, one, chips, swap, out, back):
    first_core = lax.rem(lax.axis_index("rows"), 2) == 0
    out[0] = rim[...].astype(jnp.float32)
    out[1] = far[...].astype(jnp.float32)
    out[2] = chips[1] + jnp.where(first_core, one[...], 0.0)
    back[...] = chips[0] + jnp.where(first_core, swap[...], 0.0)


def forward_kernel(
    rows, cols, live, blocks, far, back, swap, mate, own, diag, every, damage, upper_far,
    product_out, copies_out, upper, total, top, bottom, sems
):
    here = own.shape[0]
    size = diag.shape[1]
    vecs = blocks.shape[1]
    copies = streamed(upper_far, upper, sems)
    for copy in copies:
        copy.start()
    mine = lax.axis_index("rows")
    second_core = lax.rem(mine, 2) == 1
    for b in range(here):
        put_halves(top, bottom, b, blocks[b].astype(jnp.float32))
    for b in range(RIM):
        put_halves(top, bottom, here + b, jnp.where(second_core, mate[1, b], mate[0, b]))
        put_halves(top, bottom, 2 * here + b, far[b].astype(jnp.float32))
        put_halves(top, bottom, 3 * here + b, jnp.where(second_core, swap[b], mate[1, b]))
    put_halves(top, bottom, REACH * here, jnp.zeros((vecs, size), jnp.float32))
    for b in range(here):
        total[b] = own[b] + lax.dot_general(
            blocks[b], diag[b], TRANSPOSED, preferred_element_type=jnp.float32
        )
    total[:RIM] += back[...] + mate[2]

    def product(x, s):
        pair = jnp.concatenate([upper[s], upper[s + 1]], axis=1)
        return lax.dot_general(x, pair, TRANSPOSED, preferred_element_type=jnp.float32)

    first = 0
    for copy, count in zip(copies, PIECES):
        copy.wait()
        each_pair(
            first, count, live[0], lambda s: cols[s] - mine * here, lambda s: rows[s] - mine * here,
            top, bottom, total, product,
        )
        first += count
    soft = softness(damage[...])
    gram = jnp.zeros((2 * vecs, every.shape[0]), jnp.float32)
    for b in range(here):
        raw = total[b]
        cut = slice(b * size, (b + 1) * size)
        product_out[:, cut] = raw * soft[b : b + 1, :]
        high = raw.astype(jnp.bfloat16)
        low = (raw - high.astype(jnp.float32)).astype(jnp.bfloat16)
        gram += lax.dot_general(
            jnp.concatenate([high, low], 0), every[:, cut], TRANSPOSED,
            preferred_element_type=jnp.float32,
        )
    gram = gram[:vecs] + gram[vecs:]
    half = vecs // 2
    packed = jnp.concatenate([gram[:half], gram[half:]], axis=1)
    copies_out[...] = jnp.broadcast_to(packed[None], copies_out.shape)


def sum_kernel(scale, parts, out):
    packed = jnp.sum(parts[...], axis=0) * scale
    columns = out.shape[1]
    half = packed.shape[0]
    out[:half] = packed[:, :columns]
    out[half:] = packed[:, columns:]


def backward(groups, rows, cols, live, vectors, damage, upper):
    f32, bf16 = jnp.float32, jnp.bfloat16
    vecs = vectors.shape[0]
    here, size = damage.shape
    slots = upper.shape[0]
    rim = (RIM, vecs, size)
    return call(
        backward_kernel, "backward", [FAR] * 6,
        [
            ((groups, vecs, here * size), bf16), ((here, vecs, size), bf16), (rim, bf16),
            ((here, vecs, size), f32), (rim, f32), ((2,) + rim, f32), (rim, f32),
        ],
        [
            pltpu.SMEM(rows.shape, rows.dtype),
            pltpu.SMEM(cols.shape, cols.dtype),
            pltpu.SMEM(live.shape, live.dtype),
            pltpu.VMEM(vectors.shape, f32),
            pltpu.VMEM(damage.shape, f32),
            pltpu.VMEM(upper.shape, bf16),
            pltpu.VMEM((REACH * here + 1, vecs, size), f32),
            pltpu.VMEM((here + 1, 2 * vecs, size), bf16),
            pltpu.VMEM((here + 1, 2 * vecs, size), bf16),
            pltpu.SemaphoreType.DMA((len(PIECES),)),
            pltpu.SemaphoreType.DMA((5,)),
        ],
        BLOCKS_STAY, 2 * slots * vecs * size * size, 2 * slots * size * size,
    )(in_hbm(rows), in_hbm(cols), live, in_hbm(vectors), in_hbm(damage), in_hbm(upper))


def forward(
    owners, rows, cols, live, blocks, far, back, swap, mate, own, diag, every, damage, upper
):
    f32, bf16 = jnp.float32, jnp.bfloat16
    here, vecs, size = blocks.shape
    slots = upper.shape[0]
    return call(
        forward_kernel, "forward", [SM] * 3 + [VM] * 9 + [FAR],
        [((vecs, here * size), f32), ((owners, vecs // 2, 2 * every.shape[0]), f32)],
        [
            pltpu.VMEM(upper.shape, bf16),
            pltpu.VMEM((here + 1, vecs, size), f32),
            pltpu.VMEM((REACH * here + 1, 2 * vecs, size), bf16),
            pltpu.VMEM((REACH * here + 1, 2 * vecs, size), bf16),
            pltpu.SemaphoreType.DMA((len(PIECES),)),
        ],
        BLOCKS_STAY, 2 * slots * vecs * size * size, 2 * slots * size * size,
    )(rows, cols, live, blocks, far, back, swap, mate, own, diag, every, damage, in_hbm(upper))


def on_device(vectors, damage, diag_blocks, upper_blocks, block_rows, block_cols, live_slots):
    f32, bf16 = jnp.float32, jnp.bfloat16
    vecs, width = vectors.shape
    here, size = diag_blocks.shape[:2]
    owners, groups = lax.axis_size("rows"), lax.axis_size("vec")
    damage = damage.reshape(here, size)
    rim = (RIM, vecs, size)

    copies, blocks, edge, own, one, chips, swap = backward(
        groups, block_rows, block_cols, live_slots, vectors, damage, upper_blocks
    )
    every = lax.all_to_all(copies, "vec", 0, 0).reshape(groups * vecs, width)

    down = [(d, d - 2) for d in range(2, owners)]
    up = [(d, d + 2) for d in range(owners - 2)]
    across = [(d, d + 3) for d in range(1, owners - 3, 2)]
    across += [(b, a) for a, b in across]
    mates = [(d, d ^ 1) for d in range(owners)]

    far = lax.ppermute(edge, "rows", down)
    chips = lax.ppermute(chips, "rows", up)
    swap = lax.ppermute(swap, "rows", across)
    mate, back = call(
        relay_kernel, "relay", [VM] * 5, [((3,) + rim, f32), (rim, f32)], [], SMALL_VMEM,
        0, 8 * size,
    )(edge, far, one, chips, swap)
    mate = lax.ppermute(mate, "rows", mates)

    product, partials = forward(
        owners, block_rows, block_cols, live_slots, blocks, far, back, swap, mate, own, diag_blocks,
        every, damage, upper_blocks,
    )
    partials = lax.all_to_all(partials, "rows", 0, 0)
    (projected,) = call(
        functools.partial(sum_kernel, 1.0 / (width * owners)), "sum", [VM],
        [((vecs, groups * vecs), f32)], [], SMALL_VMEM, 0, partials.size * 4,
    )(partials)
    return (product, projected)


def solution(mesh):
    return jax.shard_map(
        on_device,
        mesh=mesh,
        in_specs=(
            P("vec", "rows"),
            P("rows"),
            P("rows", None, None),
            P("rows", None, None),
            P("rows"),
            P("rows"),
            P("rows"),
        ),
        out_specs=(P("vec", "rows"), P("vec", None)),
        check_vma=False,
    )
```

```python
import functools

import jax
import jax.numpy as jnp
from jax import lax
from jax.experimental import pallas as pl
from jax.experimental.pallas import tpu as pltpu
from jax.sharding import PartitionSpec as P

REACH = 4
RIM = 6
PIECES = (16, 48, 32, 32)
KEPT = 64
LATE_PIECES = (64,)
SMALL_VMEM = 8 << 20


resid_eta = 0.001

VM = pl.BlockSpec(memory_space=pltpu.VMEM)
SM = pl.BlockSpec(memory_space=pltpu.SMEM)
FAR = pl.BlockSpec(memory_space=pl.ANY)
TRANSPOSED = (((1,), (1,)), ((), ()))


def in_hbm(array):
    return pltpu.with_memory_space_constraint(array, pltpu.HBM)


def call(kernel, name, in_specs, outs, scratch, vmem, flops, moved, first_far=False):
    return pl.pallas_call(
        kernel,
        name=name,
        in_specs=in_specs,
        out_specs=[FAR if first_far and i == 0 else VM for i in range(len(outs))],
        out_shape=[jax.ShapeDtypeStruct(shape, dtype) for shape, dtype in outs],
        scratch_shapes=scratch,
        compiler_params=pltpu.CompilerParams(vmem_limit_bytes=vmem),
        cost_estimate=pl.CostEstimate(flops=flops, bytes_accessed=moved, transcendentals=0),
    )


def softness(damage):
    return jnp.sqrt((1.0 - damage) ** 2 + resid_eta)


def put_halves(top, bottom, at, x):
    z = jnp.zeros_like(x)
    top[at] = jnp.concatenate([x, z], 0).astype(jnp.bfloat16)
    bottom[at] = jnp.concatenate([z, x], 0).astype(jnp.bfloat16)


def streamed(upper_far, parts, pieces, sems):
    copies = []
    for i, (first, count) in enumerate(pieces):
        start, buffer = [part for part in parts if part[0] <= first][-1]
        copies.append(
            pltpu.make_async_copy(
                upper_far.at[pl.ds(first, count)], buffer.at[pl.ds(first - start, count)], sems.at[i]
            )
        )
    return copies


def pieces_of(first, slots, sizes):
    pieces = []
    for count in sizes:
        pieces.append((first, count))
        first += count
    assert first == slots
    return pieces


def each_pair(first, count, live, take, give, top, bottom, total, product):
    vecs = total.shape[1]
    none_from, none_to = top.shape[0] - 1, total.shape[0] - 1

    def taken(s):
        return jnp.where(s < live, take(s), none_from)

    results = []
    for s in range(first, first + count, 2):
        y = product(jnp.concatenate([top[taken(s)], bottom[taken(s + 1)]], axis=1), s)
        results += [y[:vecs], y[vecs:]]
    for k in range(count):
        s = first + k
        total[jnp.where(s < live, give(s), none_to)] += results[k]


def backward_kernel(
    rows_far, cols_far, live_far, vectors_far, damage_far, upper_far, everyones_far, blocks, rim,
    own, one, chips, swap, near, rows, cols, live, vectors, damage, flat, rest, total, top, bottom,
    sems, few_sems, out_sems
):
    here = own.shape[0]
    size = near.shape[1]
    kept = near.shape[0]
    few = [
        pltpu.make_async_copy(source, target, few_sems.at[i])
        for i, (source, target) in enumerate(
            ((vectors_far, vectors), (damage_far, damage), (rows_far, rows), (cols_far, cols),
             (live_far, live))
        )
    ]
    pieces = pieces_of(0, upper_far.shape[0], PIECES)
    copies = streamed(upper_far, ((0, near), (kept, rest)), pieces, sems)
    for copy in few + copies:
        copy.start()
    mine = lax.axis_index("rows")
    total[...] = jnp.zeros_like(total)
    for copy in few:
        copy.wait()
    soft = softness(damage[...])
    for b in range(here):
        cut = slice(b * size, (b + 1) * size)
        scaled = (vectors[:, cut] * soft[b : b + 1, :]).astype(jnp.bfloat16)
        blocks[b] = scaled
        if b < RIM:
            rim[b] = scaled
        flat[:, cut] = scaled
        put_halves(top, bottom, b, scaled.astype(jnp.float32))
    put_halves(top, bottom, here, jnp.zeros(total.shape[1:], jnp.float32))
    gifts = [
        pltpu.make_async_copy(flat, everyones_far.at[i], out_sems.at[i])
        for i in range(everyones_far.shape[0])
    ]
    for gift in gifts:
        gift.start()

    def product(x, s):
        blocks_of = near[pl.ds(s, 2)] if s < kept else rest[pl.ds(s - kept, 2)]
        return jnp.dot(x, blocks_of.reshape(2 * size, size), preferred_element_type=jnp.float32)

    for copy, (first, count) in zip(copies, pieces):
        copy.wait()
        each_pair(
            first, count, live[0], lambda s: rows[s] - mine * here, lambda s: cols[s] - mine * here,
            top, bottom, total, product,
        )
    own[...] = total[:here]
    one[...] = total[here : here + RIM]
    second_core = lax.rem(mine, 2)
    other = jnp.where(second_core == 1, here, 3 * here)
    chips[0] = total[2 * here : 2 * here + RIM]
    chips[1] = total[pl.ds(other, RIM)]
    swap[:RIM] = jnp.where(
        second_core == 1, total[3 * here : 3 * here + RIM], blocks[:RIM].astype(jnp.float32)
    )
    swap[RIM:] = jnp.zeros((swap.shape[0] - RIM,) + swap.shape[1:], jnp.float32)
    for gift in gifts:
        gift.wait()


def relay_kernel(rim, far, one, chips, swap, out, back):
    first_core = lax.rem(lax.axis_index("rows"), 2) == 0
    out[0] = rim[...].astype(jnp.float32)
    out[1] = far[...].astype(jnp.float32)
    out[2] = chips[1] + jnp.where(first_core, one[...], 0.0)
    back[...] = chips[0] + jnp.where(first_core, swap[:RIM], 0.0)


def forward_kernel(
    rows, cols, live, blocks, far, back, swap, mate, own, diag, near, upper_far, raw, rest, total,
    top, bottom, sems
):
    here = own.shape[0]
    kept = near.shape[0]
    pieces = pieces_of(kept, upper_far.shape[0], LATE_PIECES)
    copies = streamed(upper_far, ((kept, rest),), pieces, sems)
    for copy in copies:
        copy.start()
    vecs, size = blocks.shape[1:]
    mine = lax.axis_index("rows")
    second_core = lax.rem(mine, 2) == 1
    for b in range(here):
        put_halves(top, bottom, b, blocks[b].astype(jnp.float32))
    for b in range(RIM):
        put_halves(top, bottom, here + b, jnp.where(second_core, mate[1, b], mate[0, b]))
        put_halves(top, bottom, 2 * here + b, far[b].astype(jnp.float32))
        put_halves(top, bottom, 3 * here + b, jnp.where(second_core, swap[b], mate[1, b]))
    put_halves(top, bottom, REACH * here, jnp.zeros((vecs, size), jnp.float32))
    for b in range(here):
        total[b] = own[b] + lax.dot_general(
            blocks[b], diag[b], TRANSPOSED, preferred_element_type=jnp.float32
        )
    total[:RIM] += back[...] + mate[2]

    def product(x, s):
        pair = (near[s], near[s + 1]) if s < kept else (rest[s - kept], rest[s - kept + 1])
        return lax.dot_general(
            x, jnp.concatenate(pair, axis=1), TRANSPOSED, preferred_element_type=jnp.float32
        )

    for copy, (first, count) in zip([None] + copies, [(0, kept)] + pieces):
        if copy is not None:
            copy.wait()
        each_pair(
            first, count, live[0], lambda s: cols[s] - mine * here, lambda s: rows[s] - mine * here,
            top, bottom, total, product,
        )
    raw[...] = total[:here]


def finish_kernel(raws, damage, every, product_far, copies_out, product, sem):
    here, vecs, size = raws.shape
    soft = softness(damage[...])
    for b in range(here):
        product[:, b * size : (b + 1) * size] = raws[b] * soft[b : b + 1, :]
    leave = pltpu.make_async_copy(product, product_far, sem)
    leave.start()
    gram = jnp.zeros((2 * vecs, every.shape[0]), jnp.float32)
    for b in range(here):
        raw = raws[b]
        high = raw.astype(jnp.bfloat16)
        low = (raw - high.astype(jnp.float32)).astype(jnp.bfloat16)
        gram += lax.dot_general(
            jnp.concatenate([high, low], 0), every[:, b * size : (b + 1) * size], TRANSPOSED,
            preferred_element_type=jnp.float32,
        )
    gram = gram[:vecs] + gram[vecs:]
    half = vecs // 2
    packed = jnp.concatenate([gram[:half], gram[half:]], axis=1)
    copies_out[...] = jnp.broadcast_to(packed[None], copies_out.shape)
    leave.wait()


def sum_kernel(scale, parts, out):
    packed = jnp.sum(parts[...], axis=0) * scale
    columns = out.shape[1]
    half = packed.shape[0]
    out[:half] = packed[:, :columns]
    out[half:] = packed[:, columns:]


def backward(groups, rows, cols, live, vectors, damage, upper):
    f32, bf16 = jnp.float32, jnp.bfloat16
    vecs = vectors.shape[0]
    here, size = damage.shape
    slots = upper.shape[0]
    rim = (RIM, vecs, size)
    swapped = (2 * RIM + 2, vecs, size)
    return call(
        backward_kernel, "backward", [FAR] * 6,
        [
            ((groups, vecs, here * size), bf16), ((here, vecs, size), bf16), (rim, bf16),
            ((here, vecs, size), f32), (rim, f32), ((2,) + rim, f32),
            (swapped, f32), ((KEPT, size, size), bf16),
        ],
        [
            pltpu.SMEM(rows.shape, rows.dtype),
            pltpu.SMEM(cols.shape, cols.dtype),
            pltpu.SMEM(live.shape, live.dtype),
            pltpu.VMEM(vectors.shape, f32),
            pltpu.VMEM(damage.shape, f32),
            pltpu.VMEM((vecs, here * size), bf16),
            pltpu.VMEM((slots - KEPT, size, size), bf16),
            pltpu.VMEM((REACH * here + 1, vecs, size), f32),
            pltpu.VMEM((here + 1, 2 * vecs, size), bf16),
            pltpu.VMEM((here + 1, 2 * vecs, size), bf16),
            pltpu.SemaphoreType.DMA((len(PIECES),)),
            pltpu.SemaphoreType.DMA((5,)),
            pltpu.SemaphoreType.DMA((groups,)),
        ],
        SMALL_VMEM, 2 * slots * vecs * size * size, 2 * slots * size * size, True,
    )(in_hbm(rows), in_hbm(cols), live, in_hbm(vectors), in_hbm(damage), in_hbm(upper))


def forward(rows, cols, live, blocks, far, back, swap, mate, own, diag, near, upper):
    f32, bf16 = jnp.float32, jnp.bfloat16
    here, vecs, size = blocks.shape
    slots = upper.shape[0]
    return call(
        forward_kernel, "forward", [SM] * 3 + [VM] * 8 + [FAR], [((here, vecs, size), f32)],
        [
            pltpu.VMEM((slots - KEPT, size, size), bf16),
            pltpu.VMEM((here + 1, vecs, size), f32),
            pltpu.VMEM((REACH * here + 1, 2 * vecs, size), bf16),
            pltpu.VMEM((REACH * here + 1, 2 * vecs, size), bf16),
            pltpu.SemaphoreType.DMA((len(LATE_PIECES),)),
        ],
        SMALL_VMEM, 2 * slots * vecs * size * size, 2 * slots * size * size,
    )(rows, cols, live, blocks, far, back, swap, mate, own, diag, near, in_hbm(upper))


def on_device(vectors, damage, diag_blocks, upper_blocks, block_rows, block_cols, live_slots):
    f32, bf16 = jnp.float32, jnp.bfloat16
    vecs, width = vectors.shape
    here, size = diag_blocks.shape[:2]
    owners, groups = lax.axis_size("rows"), lax.axis_size("vec")
    damage = damage.reshape(here, size)
    rim = (RIM, vecs, size)

    copies, blocks, edge, own, one, chips, swap, near = backward(
        groups, block_rows, block_cols, live_slots, vectors, damage, upper_blocks
    )
    every = lax.all_to_all(copies, "vec", 0, 0).reshape(groups * vecs, width)

    down = [(d, d - 2) for d in range(2, owners)]
    up = [(d, d + 2) for d in range(owners - 2)]
    across = [(d, d + 3) for d in range(1, owners - 3, 2)]
    across += [(b, a) for a, b in across]
    mates = [(d, d ^ 1) for d in range(owners)]

    far = lax.ppermute(edge, "rows", down)
    chips = lax.ppermute(chips, "rows", up)
    swap = lax.ppermute(swap, "rows", across)
    mate, back = call(
        relay_kernel, "relay", [VM] * 5, [((3,) + rim, f32), (rim, f32)], [], SMALL_VMEM,
        0, 8 * size,
    )(edge, far, one, chips, swap)
    mate = lax.ppermute(mate, "rows", mates)

    (raw,) = forward(
        block_rows, block_cols, live_slots, blocks, far, back, swap, mate, own, diag_blocks, near,
        upper_blocks,
    )
    product, partials = call(
        finish_kernel, "finish", [VM] * 3,
        [((vecs, width), f32), ((owners, vecs // 2, 2 * groups * vecs), f32)],
        [pltpu.VMEM((vecs, width), f32), pltpu.SemaphoreType.DMA(())],
        SMALL_VMEM, 0, 8 * vecs * width, True,
    )(raw, damage, every)
    partials = lax.all_to_all(partials, "rows", 0, 0)
    (projected,) = call(
        functools.partial(sum_kernel, 1.0 / (width * owners)), "sum", [VM],
        [((vecs, groups * vecs), f32)], [], SMALL_VMEM, 0, partials.size * 4,
    )(partials)
    return (product, projected)


def solution(mesh):
    return jax.shard_map(
        on_device,
        mesh=mesh,
        in_specs=(
            P("vec", "rows"),
            P("rows"),
            P("rows", None, None),
            P("rows", None, None),
            P("rows"),
            P("rows"),
            P("rows"),
        ),
        out_specs=(P("vec", "rows"), P("vec", None)),
        check_vma=False,
    )
```

```python
import functools

import jax
import jax.numpy as jnp
from jax import lax
from jax.experimental import pallas as pl
from jax.experimental.pallas import tpu as pltpu
from jax.sharding import PartitionSpec as P

REACH = 4
RIM = 6
PIECES = (32, 32, 32, 32)
LATE_PIECES = (64, 64)
SMALL_VMEM = 8 << 20
BLOCKS_STAY = 16 << 20


resid_eta = 0.001

VM = pl.BlockSpec(memory_space=pltpu.VMEM)
SM = pl.BlockSpec(memory_space=pltpu.SMEM)
FAR = pl.BlockSpec(memory_space=pl.ANY)
TRANSPOSED = (((1,), (1,)), ((), ()))


def in_hbm(array):
    return pltpu.with_memory_space_constraint(array, pltpu.HBM)


def call(kernel, name, in_specs, outs, scratch, vmem, flops, moved):
    return pl.pallas_call(
        kernel,
        name=name,
        in_specs=in_specs,
        out_specs=[FAR if i == 0 else VM for i in range(len(outs))] if scratch else [VM] * len(outs),
        out_shape=[jax.ShapeDtypeStruct(shape, dtype) for shape, dtype in outs],
        scratch_shapes=scratch,
        compiler_params=pltpu.CompilerParams(vmem_limit_bytes=vmem),
        cost_estimate=pl.CostEstimate(flops=flops, bytes_accessed=moved, transcendentals=0),
    )


def softness(damage):
    return jnp.sqrt((1.0 - damage) ** 2 + resid_eta)


def put_halves(top, bottom, at, x):
    z = jnp.zeros_like(x)
    top[at] = jnp.concatenate([x, z], 0).astype(jnp.bfloat16)
    bottom[at] = jnp.concatenate([z, x], 0).astype(jnp.bfloat16)


def streamed(upper_far, upper, sems, pieces):
    copies, first = [], 0
    for i, count in enumerate(pieces):
        cut = pl.ds(first, count)
        copies.append(pltpu.make_async_copy(upper_far.at[cut], upper.at[cut], sems.at[i]))
        first += count
    assert first == upper.shape[0]
    return copies


def each_pair(first, count, live, take, give, top, bottom, total, product):
    vecs = total.shape[1]
    none_from, none_to = top.shape[0] - 1, total.shape[0] - 1

    def taken(s):
        return jnp.where(s < live, take(s), none_from)

    results = []
    for s in range(first, first + count, 2):
        y = product(jnp.concatenate([top[taken(s)], bottom[taken(s + 1)]], axis=1), s)
        results += [y[:vecs], y[vecs:]]
    for k in range(count):
        s = first + k
        total[jnp.where(s < live, give(s), none_to)] += results[k]


def backward_kernel(
    rows_far, cols_far, live_far, vectors_far, damage_far, upper_far, everyones_far, blocks, rim,
    own, one, chips, swap, rows, cols, live, vectors, damage, flat, upper, total, top, bottom, sems,
    few_sems, out_sems
):
    here = own.shape[0]
    size = upper.shape[1]
    few = [
        pltpu.make_async_copy(source, target, few_sems.at[i])
        for i, (source, target) in enumerate(
            ((vectors_far, vectors), (damage_far, damage), (rows_far, rows), (cols_far, cols),
             (live_far, live))
        )
    ]
    copies = streamed(upper_far, upper, sems, PIECES)
    for copy in few + copies:
        copy.start()
    mine = lax.axis_index("rows")
    total[...] = jnp.zeros_like(total)
    for copy in few:
        copy.wait()
    soft = softness(damage[...])
    for b in range(here):
        cut = slice(b * size, (b + 1) * size)
        scaled = (vectors[:, cut] * soft[b : b + 1, :]).astype(jnp.bfloat16)
        blocks[b] = scaled
        if b < RIM:
            rim[b] = scaled
        flat[:, cut] = scaled
        put_halves(top, bottom, b, scaled.astype(jnp.float32))
    put_halves(top, bottom, here, jnp.zeros(total.shape[1:], jnp.float32))
    gifts = [
        pltpu.make_async_copy(flat, everyones_far.at[i], out_sems.at[i])
        for i in range(everyones_far.shape[0])
    ]
    for gift in gifts:
        gift.start()

    def product(x, s):
        pair = upper[pl.ds(s, 2)].reshape(2 * size, size)
        return jnp.dot(x, pair, preferred_element_type=jnp.float32)

    first = 0
    for copy, count in zip(copies, PIECES):
        copy.wait()
        each_pair(
            first, count, live[0], lambda s: rows[s] - mine * here, lambda s: cols[s] - mine * here,
            top, bottom, total, product,
        )
        first += count
    own[...] = total[:here]
    one[...] = total[here : here + RIM]
    second_core = lax.rem(mine, 2)
    other = jnp.where(second_core == 1, here, 3 * here)
    chips[0] = total[2 * here : 2 * here + RIM]
    chips[1] = total[pl.ds(other, RIM)]
    swap[...] = jnp.where(
        second_core == 1, total[3 * here : 3 * here + RIM], blocks[:RIM].astype(jnp.float32)
    )
    for gift in gifts:
        gift.wait()


def relay_kernel(rim, far, one, chips, swap, out, back):
    first_core = lax.rem(lax.axis_index("rows"), 2) == 0
    out[0] = rim[...].astype(jnp.float32)
    out[1] = far[...].astype(jnp.float32)
    out[2] = chips[1] + jnp.where(first_core, one[...], 0.0)
    back[...] = chips[0] + jnp.where(first_core, swap[...], 0.0)


def forward_kernel(
    rows, cols, live, blocks, far, back, swap, mate, own, diag, every, damage, upper_far,
    product_far, copies_out, product_near, upper, total, top, bottom, sems, out_sem
):
    here = own.shape[0]
    size = diag.shape[1]
    vecs = blocks.shape[1]
    copies = streamed(upper_far, upper, sems, LATE_PIECES)
    for copy in copies:
        copy.start()
    mine = lax.axis_index("rows")
    second_core = lax.rem(mine, 2) == 1
    for b in range(here):
        put_halves(top, bottom, b, blocks[b].astype(jnp.float32))
    for b in range(RIM):
        put_halves(top, bottom, here + b, jnp.where(second_core, mate[1, b], mate[0, b]))
        put_halves(top, bottom, 2 * here + b, far[b].astype(jnp.float32))
        put_halves(top, bottom, 3 * here + b, jnp.where(second_core, swap[b], mate[1, b]))
    put_halves(top, bottom, REACH * here, jnp.zeros((vecs, size), jnp.float32))
    for b in range(here):
        total[b] = own[b] + lax.dot_general(
            blocks[b], diag[b], TRANSPOSED, preferred_element_type=jnp.float32
        )
    total[:RIM] += back[...] + mate[2]

    def product(x, s):
        pair = jnp.concatenate([upper[s], upper[s + 1]], axis=1)
        return lax.dot_general(x, pair, TRANSPOSED, preferred_element_type=jnp.float32)

    first = 0
    for copy, count in zip(copies, LATE_PIECES):
        copy.wait()
        each_pair(
            first, count, live[0], lambda s: cols[s] - mine * here, lambda s: rows[s] - mine * here,
            top, bottom, total, product,
        )
        first += count
    soft = softness(damage[...])
    for b in range(here):
        product_near[:, b * size : (b + 1) * size] = total[b] * soft[b : b + 1, :]
    leave = pltpu.make_async_copy(product_near, product_far, out_sem)
    leave.start()
    gram = jnp.zeros((2 * vecs, every.shape[0]), jnp.float32)
    for b in range(here):
        raw = total[b]
        high = raw.astype(jnp.bfloat16)
        low = (raw - high.astype(jnp.float32)).astype(jnp.bfloat16)
        gram += lax.dot_general(
            jnp.concatenate([high, low], 0), every[:, b * size : (b + 1) * size], TRANSPOSED,
            preferred_element_type=jnp.float32,
        )
    gram = gram[:vecs] + gram[vecs:]
    half = vecs // 2
    packed = jnp.concatenate([gram[:half], gram[half:]], axis=1)
    copies_out[...] = jnp.broadcast_to(packed[None], copies_out.shape)
    leave.wait()


def sum_kernel(scale, parts, out):
    packed = jnp.sum(parts[...], axis=0) * scale
    columns = out.shape[1]
    half = packed.shape[0]
    out[:half] = packed[:, :columns]
    out[half:] = packed[:, columns:]


def backward(groups, rows, cols, live, vectors, damage, upper):
    f32, bf16 = jnp.float32, jnp.bfloat16
    vecs = vectors.shape[0]
    here, size = damage.shape
    slots = upper.shape[0]
    rim = (RIM, vecs, size)
    return call(
        backward_kernel, "backward", [FAR] * 6,
        [
            ((groups, vecs, here * size), bf16), ((here, vecs, size), bf16), (rim, bf16),
            ((here, vecs, size), f32), (rim, f32), ((2,) + rim, f32), (rim, f32),
        ],
        [
            pltpu.SMEM(rows.shape, rows.dtype),
            pltpu.SMEM(cols.shape, cols.dtype),
            pltpu.SMEM(live.shape, live.dtype),
            pltpu.VMEM(vectors.shape, f32),
            pltpu.VMEM(damage.shape, f32),
            pltpu.VMEM((vecs, here * size), bf16),
            pltpu.VMEM(upper.shape, bf16),
            pltpu.VMEM((REACH * here + 1, vecs, size), f32),
            pltpu.VMEM((here + 1, 2 * vecs, size), bf16),
            pltpu.VMEM((here + 1, 2 * vecs, size), bf16),
            pltpu.SemaphoreType.DMA((len(PIECES),)),
            pltpu.SemaphoreType.DMA((5,)),
            pltpu.SemaphoreType.DMA((groups,)),
        ],
        BLOCKS_STAY, 2 * slots * vecs * size * size, 2 * slots * size * size,
    )(in_hbm(rows), in_hbm(cols), live, in_hbm(vectors), in_hbm(damage), in_hbm(upper))


def forward(
    owners, rows, cols, live, blocks, far, back, swap, mate, own, diag, every, damage, upper
):
    f32, bf16 = jnp.float32, jnp.bfloat16
    here, vecs, size = blocks.shape
    slots = upper.shape[0]
    return call(
        forward_kernel, "forward", [SM] * 3 + [VM] * 9 + [FAR],
        [((vecs, here * size), f32), ((owners, vecs // 2, 2 * every.shape[0]), f32)],
        [
            pltpu.VMEM((vecs, here * size), f32),
            pltpu.VMEM(upper.shape, bf16),
            pltpu.VMEM((here + 1, vecs, size), f32),
            pltpu.VMEM((REACH * here + 1, 2 * vecs, size), bf16),
            pltpu.VMEM((REACH * here + 1, 2 * vecs, size), bf16),
            pltpu.SemaphoreType.DMA((len(LATE_PIECES),)),
            pltpu.SemaphoreType.DMA(()),
        ],
        BLOCKS_STAY, 2 * slots * vecs * size * size, 2 * slots * size * size,
    )(rows, cols, live, blocks, far, back, swap, mate, own, diag, every, damage, in_hbm(upper))


def on_device(vectors, damage, diag_blocks, upper_blocks, block_rows, block_cols, live_slots):
    f32, bf16 = jnp.float32, jnp.bfloat16
    vecs, width = vectors.shape
    here, size = diag_blocks.shape[:2]
    owners, groups = lax.axis_size("rows"), lax.axis_size("vec")
    damage = damage.reshape(here, size)
    rim = (RIM, vecs, size)

    copies, blocks, edge, own, one, chips, swap = backward(
        groups, block_rows, block_cols, live_slots, vectors, damage, upper_blocks
    )
    every = lax.all_to_all(copies, "vec", 0, 0).reshape(groups * vecs, width)

    down = [(d, d - 2) for d in range(2, owners)]
    up = [(d, d + 2) for d in range(owners - 2)]
    across = [(d, d + 3) for d in range(1, owners - 3, 2)]
    across += [(b, a) for a, b in across]
    mates = [(d, d ^ 1) for d in range(owners)]

    far = lax.ppermute(edge, "rows", down)
    chips = lax.ppermute(chips, "rows", up)
    swap = lax.ppermute(swap, "rows", across)
    mate, back = call(
        relay_kernel, "relay", [VM] * 5, [((3,) + rim, f32), (rim, f32)], [], SMALL_VMEM,
        0, 8 * size,
    )(edge, far, one, chips, swap)
    mate = lax.ppermute(mate, "rows", mates)

    product, partials = forward(
        owners, block_rows, block_cols, live_slots, blocks, far, back, swap, mate, own, diag_blocks,
        every, damage, upper_blocks,
    )
    partials = lax.all_to_all(partials, "rows", 0, 0)
    (projected,) = call(
        functools.partial(sum_kernel, 1.0 / (width * owners)), "sum", [VM],
        [((vecs, groups * vecs), f32)], [], SMALL_VMEM, 0, partials.size * 4,
    )(partials)
    return (product, projected)


def solution(mesh):
    return jax.shard_map(
        on_device,
        mesh=mesh,
        in_specs=(
            P("vec", "rows"),
            P("rows"),
            P("rows", None, None),
            P("rows", None, None),
            P("rows"),
            P("rows"),
            P("rows"),
        ),
        out_specs=(P("vec", "rows"), P("vec", None)),
        check_vma=False,
    )
```

```python
import functools

import jax
import jax.numpy as jnp
from jax import lax
from jax.experimental import pallas as pl
from jax.experimental.pallas import tpu as pltpu
from jax.sharding import PartitionSpec as P

REACH = 4
RIM = 6
PIECES = (32, 32, 32, 32)
LATE_PIECES = (64, 64)
SMALL_VMEM = 8 << 20
BLOCKS_STAY = 16 << 20


resid_eta = 0.001

VM = pl.BlockSpec(memory_space=pltpu.VMEM)
SM = pl.BlockSpec(memory_space=pltpu.SMEM)
FAR = pl.BlockSpec(memory_space=pl.ANY)
TRANSPOSED = (((1,), (1,)), ((), ()))


def in_hbm(array):
    return pltpu.with_memory_space_constraint(array, pltpu.HBM)


def call(kernel, name, in_specs, outs, scratch, vmem, flops, moved):
    return pl.pallas_call(
        kernel,
        name=name,
        in_specs=in_specs,
        out_specs=[FAR if i == 0 else VM for i in range(len(outs))] if scratch else [VM] * len(outs),
        out_shape=[jax.ShapeDtypeStruct(shape, dtype) for shape, dtype in outs],
        scratch_shapes=scratch,
        compiler_params=pltpu.CompilerParams(vmem_limit_bytes=vmem),
        cost_estimate=pl.CostEstimate(flops=flops, bytes_accessed=moved, transcendentals=0),
    )


def softness(damage):
    return jnp.sqrt((1.0 - damage) ** 2 + resid_eta)


def put_halves(top, bottom, at, x):
    z = jnp.zeros_like(x)
    top[at] = jnp.concatenate([x, z], 0).astype(jnp.bfloat16)
    bottom[at] = jnp.concatenate([z, x], 0).astype(jnp.bfloat16)


def streamed(upper_far, upper, sems, pieces):
    copies, first = [], 0
    for i, count in enumerate(pieces):
        cut = pl.ds(first, count)
        copies.append(pltpu.make_async_copy(upper_far.at[cut], upper.at[cut], sems.at[i]))
        first += count
    assert first == upper.shape[0]
    return copies


def each_pair(first, count, live, take, give, top, bottom, total, product):
    vecs = total.shape[1]
    none_from, none_to = top.shape[0] - 1, total.shape[0] - 1

    def taken(s):
        return jnp.where(s < live, take(s), none_from)

    results = []
    for s in range(first, first + count, 2):
        y = product(jnp.concatenate([top[taken(s)], bottom[taken(s + 1)]], axis=1), s)
        results += [y[:vecs], y[vecs:]]
    for k in range(count):
        s = first + k
        total[jnp.where(s < live, give(s), none_to)] += results[k]


def backward_kernel(
    rows_far, cols_far, live_far, vectors_far, damage_far, upper_far, everyones_far, blocks, rim,
    own, one, chips, swap, rows, cols, live, vectors, damage, flat, upper, total, top, bottom, sems,
    few_sems, out_sems
):
    here = own.shape[0]
    size = upper.shape[1]
    few = [
        pltpu.make_async_copy(source, target, few_sems.at[i])
        for i, (source, target) in enumerate(
            ((vectors_far, vectors), (damage_far, damage), (rows_far, rows), (cols_far, cols),
             (live_far, live))
        )
    ]
    copies = streamed(upper_far, upper, sems, PIECES)
    for copy in few + copies:
        copy.start()
    mine = lax.axis_index("rows")
    total[...] = jnp.zeros_like(total)
    for copy in few:
        copy.wait()
    soft = softness(damage[...])
    for b in range(here):
        cut = slice(b * size, (b + 1) * size)
        scaled = (vectors[:, cut] * soft[b : b + 1, :]).astype(jnp.bfloat16)
        blocks[b] = scaled
        if b < RIM:
            rim[b] = scaled
        flat[:, cut] = scaled
        put_halves(top, bottom, b, scaled.astype(jnp.float32))
    put_halves(top, bottom, here, jnp.zeros(total.shape[1:], jnp.float32))
    gifts = [
        pltpu.make_async_copy(flat, everyones_far.at[i], out_sems.at[i])
        for i in range(everyones_far.shape[0])
    ]
    for gift in gifts:
        gift.start()

    def product(x, s):
        pair = upper[pl.ds(s, 2)].reshape(2 * size, size)
        return jnp.dot(x, pair, preferred_element_type=jnp.float32)

    first = 0
    for copy, count in zip(copies, PIECES):
        copy.wait()
        each_pair(
            first, count, live[0], lambda s: rows[s] - mine * here, lambda s: cols[s] - mine * here,
            top, bottom, total, product,
        )
        first += count
    own[...] = total[:here]
    one[...] = total[here : here + RIM]
    second_core = lax.rem(mine, 2)
    other = jnp.where(second_core == 1, here, 3 * here)
    chips[0] = total[2 * here : 2 * here + RIM]
    chips[1] = total[pl.ds(other, RIM)]
    swap[...] = jnp.where(
        second_core == 1, total[3 * here : 3 * here + RIM], blocks[:RIM].astype(jnp.float32)
    )
    for gift in gifts:
        gift.wait()


def diagonal_kernel(blocks, diag, own, out):
    for b in range(own.shape[0]):
        out[b] = own[b] + lax.dot_general(
            blocks[b], diag[b], TRANSPOSED, preferred_element_type=jnp.float32
        )


def relay_kernel(rim, far, one, chips, swap, out, back):
    first_core = lax.rem(lax.axis_index("rows"), 2) == 0
    out[0] = rim[...].astype(jnp.float32)
    out[1] = far[...].astype(jnp.float32)
    out[2] = chips[1] + jnp.where(first_core, one[...], 0.0)
    back[...] = chips[0] + jnp.where(first_core, swap[...], 0.0)


def forward_kernel(
    rows, cols, live, blocks, far, back, swap, mate, own, every, damage, upper_far,
    product_far, copies_out, product_near, upper, total, top, bottom, sems, out_sem
):
    here = own.shape[0]
    vecs, size = blocks.shape[1:]
    copies = streamed(upper_far, upper, sems, LATE_PIECES)
    for copy in copies:
        copy.start()
    mine = lax.axis_index("rows")
    second_core = lax.rem(mine, 2) == 1
    for b in range(here):
        put_halves(top, bottom, b, blocks[b].astype(jnp.float32))
    for b in range(RIM):
        put_halves(top, bottom, here + b, jnp.where(second_core, mate[1, b], mate[0, b]))
        put_halves(top, bottom, 2 * here + b, far[b].astype(jnp.float32))
        put_halves(top, bottom, 3 * here + b, jnp.where(second_core, swap[b], mate[1, b]))
    put_halves(top, bottom, REACH * here, jnp.zeros((vecs, size), jnp.float32))
    total[:here] = own[...]
    total[:RIM] += back[...] + mate[2]

    def product(x, s):
        pair = jnp.concatenate([upper[s], upper[s + 1]], axis=1)
        return lax.dot_general(x, pair, TRANSPOSED, preferred_element_type=jnp.float32)

    first = 0
    for copy, count in zip(copies, LATE_PIECES):
        copy.wait()
        each_pair(
            first, count, live[0], lambda s: cols[s] - mine * here, lambda s: rows[s] - mine * here,
            top, bottom, total, product,
        )
        first += count
    soft = softness(damage[...])
    for b in range(here):
        product_near[:, b * size : (b + 1) * size] = total[b] * soft[b : b + 1, :]
    leave = pltpu.make_async_copy(product_near, product_far, out_sem)
    leave.start()
    gram = jnp.zeros((2 * vecs, every.shape[0]), jnp.float32)
    for b in range(here):
        raw = total[b]
        high = raw.astype(jnp.bfloat16)
        low = (raw - high.astype(jnp.float32)).astype(jnp.bfloat16)
        gram += lax.dot_general(
            jnp.concatenate([high, low], 0), every[:, b * size : (b + 1) * size], TRANSPOSED,
            preferred_element_type=jnp.float32,
        )
    gram = gram[:vecs] + gram[vecs:]
    half = vecs // 2
    packed = jnp.concatenate([gram[:half], gram[half:]], axis=1)
    copies_out[...] = jnp.broadcast_to(packed[None], copies_out.shape)
    leave.wait()


def sum_kernel(scale, parts, out):
    packed = jnp.sum(parts[...], axis=0) * scale
    columns = out.shape[1]
    half = packed.shape[0]
    out[:half] = packed[:, :columns]
    out[half:] = packed[:, columns:]


def backward(groups, rows, cols, live, vectors, damage, upper):
    f32, bf16 = jnp.float32, jnp.bfloat16
    vecs = vectors.shape[0]
    here, size = damage.shape
    slots = upper.shape[0]
    rim = (RIM, vecs, size)
    return call(
        backward_kernel, "backward", [FAR] * 6,
        [
            ((groups, vecs, here * size), bf16), ((here, vecs, size), bf16), (rim, bf16),
            ((here, vecs, size), f32), (rim, f32), ((2,) + rim, f32), (rim, f32),
        ],
        [
            pltpu.SMEM(rows.shape, rows.dtype),
            pltpu.SMEM(cols.shape, cols.dtype),
            pltpu.SMEM(live.shape, live.dtype),
            pltpu.VMEM(vectors.shape, f32),
            pltpu.VMEM(damage.shape, f32),
            pltpu.VMEM((vecs, here * size), bf16),
            pltpu.VMEM(upper.shape, bf16),
            pltpu.VMEM((REACH * here + 1, vecs, size), f32),
            pltpu.VMEM((here + 1, 2 * vecs, size), bf16),
            pltpu.VMEM((here + 1, 2 * vecs, size), bf16),
            pltpu.SemaphoreType.DMA((len(PIECES),)),
            pltpu.SemaphoreType.DMA((5,)),
            pltpu.SemaphoreType.DMA((groups,)),
        ],
        BLOCKS_STAY, 2 * slots * vecs * size * size, 2 * slots * size * size,
    )(in_hbm(rows), in_hbm(cols), live, in_hbm(vectors), in_hbm(damage), in_hbm(upper))


def forward(
    owners, rows, cols, live, blocks, far, back, swap, mate, own, every, damage, upper
):
    f32, bf16 = jnp.float32, jnp.bfloat16
    here, vecs, size = blocks.shape
    slots = upper.shape[0]
    return call(
        forward_kernel, "forward", [SM] * 3 + [VM] * 8 + [FAR],
        [((vecs, here * size), f32), ((owners, vecs // 2, 2 * every.shape[0]), f32)],
        [
            pltpu.VMEM((vecs, here * size), f32),
            pltpu.VMEM(upper.shape, bf16),
            pltpu.VMEM((here + 1, vecs, size), f32),
            pltpu.VMEM((REACH * here + 1, 2 * vecs, size), bf16),
            pltpu.VMEM((REACH * here + 1, 2 * vecs, size), bf16),
            pltpu.SemaphoreType.DMA((len(LATE_PIECES),)),
            pltpu.SemaphoreType.DMA(()),
        ],
        BLOCKS_STAY, 2 * slots * vecs * size * size, 2 * slots * size * size,
    )(rows, cols, live, blocks, far, back, swap, mate, own, every, damage, in_hbm(upper))


def on_device(vectors, damage, diag_blocks, upper_blocks, block_rows, block_cols, live_slots):
    f32, bf16 = jnp.float32, jnp.bfloat16
    vecs, width = vectors.shape
    here, size = diag_blocks.shape[:2]
    owners, groups = lax.axis_size("rows"), lax.axis_size("vec")
    damage = damage.reshape(here, size)
    rim = (RIM, vecs, size)

    copies, blocks, edge, own, one, chips, swap = backward(
        groups, block_rows, block_cols, live_slots, vectors, damage, upper_blocks
    )
    every = lax.all_to_all(copies, "vec", 0, 0).reshape(groups * vecs, width)

    down = [(d, d - 2) for d in range(2, owners)]
    up = [(d, d + 2) for d in range(owners - 2)]
    across = [(d, d + 3) for d in range(1, owners - 3, 2)]
    across += [(b, a) for a, b in across]
    mates = [(d, d ^ 1) for d in range(owners)]

    far = lax.ppermute(edge, "rows", down)
    chips = lax.ppermute(chips, "rows", up)
    swap = lax.ppermute(swap, "rows", across)
    (own,) = call(
        diagonal_kernel, "diagonal", [VM] * 3, [(own.shape, f32)], [], SMALL_VMEM,
        2 * diag_blocks.size * vecs, 2 * diag_blocks.size,
    )(blocks, diag_blocks, own)
    mate, back = call(
        relay_kernel, "relay", [VM] * 5, [((3,) + rim, f32), (rim, f32)], [], SMALL_VMEM,
        0, 8 * size,
    )(edge, far, one, chips, swap)
    mate = lax.ppermute(mate, "rows", mates)

    product, partials = forward(
        owners, block_rows, block_cols, live_slots, blocks, far, back, swap, mate, own, every,
        damage, upper_blocks,
    )
    partials = lax.all_to_all(partials, "rows", 0, 0)
    (projected,) = call(
        functools.partial(sum_kernel, 1.0 / (width * owners)), "sum", [VM],
        [((vecs, groups * vecs), f32)], [], SMALL_VMEM, 0, partials.size * 4,
    )(partials)
    return (product, projected)


def solution(mesh):
    return jax.shard_map(
        on_device,
        mesh=mesh,
        in_specs=(
            P("vec", "rows"),
            P("rows"),
            P("rows", None, None),
            P("rows", None, None),
            P("rows"),
            P("rows"),
            P("rows"),
        ),
        out_specs=(P("vec", "rows"), P("vec", None)),
        check_vma=False,
    )
```

```python
import functools

import jax
import jax.numpy as jnp
from jax import lax
from jax.experimental import pallas as pl
from jax.experimental.pallas import tpu as pltpu
from jax.sharding import PartitionSpec as P

REACH = 4
RIM = 6
PIECES = (32, 32, 32, 32)
LATE_PIECES = (64, 64)
SMALL_VMEM = 8 << 20
BLOCKS_STAY = 16 << 20


resid_eta = 0.001

VM = pl.BlockSpec(memory_space=pltpu.VMEM)
SM = pl.BlockSpec(memory_space=pltpu.SMEM)
FAR = pl.BlockSpec(memory_space=pl.ANY)
TRANSPOSED = (((1,), (1,)), ((), ()))


def in_hbm(array):
    return pltpu.with_memory_space_constraint(array, pltpu.HBM)


def call(kernel, name, in_specs, outs, scratch, vmem, flops, moved):
    return pl.pallas_call(
        kernel,
        name=name,
        in_specs=in_specs,
        out_specs=[FAR if i == 0 else VM for i in range(len(outs))] if scratch else [VM] * len(outs),
        out_shape=[jax.ShapeDtypeStruct(shape, dtype) for shape, dtype in outs],
        scratch_shapes=scratch,
        compiler_params=pltpu.CompilerParams(vmem_limit_bytes=vmem),
        cost_estimate=pl.CostEstimate(flops=flops, bytes_accessed=moved, transcendentals=0),
    )


def softness(damage):
    return jnp.sqrt((1.0 - damage) ** 2 + resid_eta)


def put_halves(top, bottom, at, x):
    z = jnp.zeros_like(x)
    top[at] = jnp.concatenate([x, z], 0).astype(jnp.bfloat16)
    bottom[at] = jnp.concatenate([z, x], 0).astype(jnp.bfloat16)


def streamed(upper_far, upper, sems, pieces):
    copies, first = [], 0
    for i, count in enumerate(pieces):
        cut = pl.ds(first, count)
        copies.append(pltpu.make_async_copy(upper_far.at[cut], upper.at[cut], sems.at[i]))
        first += count
    assert first == upper.shape[0]
    return copies


def each_pair(first, count, live, take, give, top, bottom, total, product):
    vecs = total.shape[1]
    none_from, none_to = top.shape[0] - 1, total.shape[0] - 1

    def taken(s):
        return jnp.where(s < live, take(s), none_from)

    results = []
    for s in range(first, first + count, 2):
        y = product(jnp.concatenate([top[taken(s)], bottom[taken(s + 1)]], axis=1), s)
        results += [y[:vecs], y[vecs:]]
    for k in range(count):
        s = first + k
        total[jnp.where(s < live, give(s), none_to)] += results[k]


def backward_kernel(
    rows_far, cols_far, live_far, vectors_far, damage_far, upper_far, everyones_far, blocks, rim,
    own, one, chips, swap, rows, cols, live, vectors, damage, flat, upper, total, top, bottom, sems,
    few_sems, out_sems
):
    here = own.shape[0]
    size = upper.shape[1]
    few = [
        pltpu.make_async_copy(source, target, few_sems.at[i])
        for i, (source, target) in enumerate(
            ((vectors_far, vectors), (damage_far, damage), (rows_far, rows), (cols_far, cols),
             (live_far, live))
        )
    ]
    copies = streamed(upper_far, upper, sems, PIECES)
    for copy in few + copies:
        copy.start()
    mine = lax.axis_index("rows")
    total[...] = jnp.zeros_like(total)
    for copy in few:
        copy.wait()
    soft = softness(damage[...])
    for b in range(here):
        cut = slice(b * size, (b + 1) * size)
        scaled = (vectors[:, cut] * soft[b : b + 1, :]).astype(jnp.bfloat16)
        blocks[b] = scaled
        if b < RIM:
            rim[b] = scaled
        flat[:, cut] = scaled
        put_halves(top, bottom, b, scaled.astype(jnp.float32))
    put_halves(top, bottom, here, jnp.zeros(total.shape[1:], jnp.float32))
    gifts = [
        pltpu.make_async_copy(flat, everyones_far.at[i], out_sems.at[i])
        for i in range(everyones_far.shape[0])
    ]
    for gift in gifts:
        gift.start()

    def product(x, s):
        pair = upper[pl.ds(s, 2)].reshape(2 * size, size)
        return jnp.dot(x, pair, preferred_element_type=jnp.float32)

    first = 0
    for copy, count in zip(copies, PIECES):
        copy.wait()
        each_pair(
            first, count, live[0], lambda s: rows[s] - mine * here, lambda s: cols[s] - mine * here,
            top, bottom, total, product,
        )
        first += count
    own[...] = total[:here]
    one[...] = total[here : here + RIM]
    second_core = lax.rem(mine, 2)
    other = jnp.where(second_core == 1, here, 3 * here)
    chips[0] = total[2 * here : 2 * here + RIM]
    chips[1] = total[pl.ds(other, RIM)]
    swap[...] = jnp.where(
        second_core == 1, total[3 * here : 3 * here + RIM], blocks[:RIM].astype(jnp.float32)
    )
    for gift in gifts:
        gift.wait()


def relay_kernel(rim, far, one, chips, swap, out, back):
    first_core = lax.rem(lax.axis_index("rows"), 2) == 0
    out[0] = rim[...].astype(jnp.float32)
    out[1] = far[...].astype(jnp.float32)
    out[2] = chips[1] + jnp.where(first_core, one[...], 0.0)
    back[...] = chips[0] + jnp.where(first_core, swap[...], 0.0)


def forward_kernel(
    rows, cols, live, blocks, far, back, swap, mate, own, diag, every, damage, upper_far,
    product_far, copies_out, product_near, upper, total, top, bottom, sems, out_sem
):
    here = own.shape[0]
    size = diag.shape[1]
    vecs = blocks.shape[1]
    copies = streamed(upper_far, upper, sems, LATE_PIECES)
    for copy in copies:
        copy.start()
    mine = lax.axis_index("rows")
    second_core = lax.rem(mine, 2) == 1
    for b in range(here):
        put_halves(top, bottom, b, blocks[b].astype(jnp.float32))
    for b in range(RIM):
        put_halves(top, bottom, here + b, jnp.where(second_core, mate[1, b], mate[0, b]))
        put_halves(top, bottom, 2 * here + b, far[b].astype(jnp.float32))
        put_halves(top, bottom, 3 * here + b, jnp.where(second_core, swap[b], mate[1, b]))
    put_halves(top, bottom, REACH * here, jnp.zeros((vecs, size), jnp.float32))
    for b in range(here):
        total[b] = own[b] + lax.dot_general(
            blocks[b], diag[b], TRANSPOSED, preferred_element_type=jnp.float32
        )
    total[:RIM] += back[...] + mate[2]

    def product(x, s):
        pair = jnp.concatenate([upper[s], upper[s + 1]], axis=1)
        return lax.dot_general(x, pair, TRANSPOSED, preferred_element_type=jnp.float32)

    first = 0
    for copy, count in zip(copies, LATE_PIECES):
        copy.wait()
        each_pair(
            first, count, live[0], lambda s: cols[s] - mine * here, lambda s: rows[s] - mine * here,
            top, bottom, total, product,
        )
        first += count
    soft = softness(damage[...])
    for b in range(here):
        product_near[:, b * size : (b + 1) * size] = total[b] * soft[b : b + 1, :]
    leave = pltpu.make_async_copy(product_near, product_far, out_sem)
    leave.start()
    gram = jnp.zeros((2 * vecs, every.shape[0]), jnp.float32)
    for b in range(here):
        raw = total[b]
        high = raw.astype(jnp.bfloat16)
        low = (raw - high.astype(jnp.float32)).astype(jnp.bfloat16)
        gram += lax.dot_general(
            jnp.concatenate([high, low], 0), every[:, b * size : (b + 1) * size], TRANSPOSED,
            preferred_element_type=jnp.float32,
        )
    gram = gram[:vecs] + gram[vecs:]
    half = vecs // 2
    packed = jnp.concatenate([gram[:half], gram[half:]], axis=1)
    copies_out[...] = jnp.broadcast_to(packed.astype(copies_out.dtype)[None], copies_out.shape)
    leave.wait()


def sum_kernel(scale, parts, out):
    packed = jnp.sum(parts[...].astype(jnp.float32), axis=0) * scale
    columns = out.shape[1]
    half = packed.shape[0]
    out[:half] = packed[:, :columns]
    out[half:] = packed[:, columns:]


def backward(groups, rows, cols, live, vectors, damage, upper):
    f32, bf16 = jnp.float32, jnp.bfloat16
    vecs = vectors.shape[0]
    here, size = damage.shape
    slots = upper.shape[0]
    rim = (RIM, vecs, size)
    return call(
        backward_kernel, "backward", [FAR] * 6,
        [
            ((groups, vecs, here * size), bf16), ((here, vecs, size), bf16), (rim, bf16),
            ((here, vecs, size), f32), (rim, f32), ((2,) + rim, f32), (rim, f32),
        ],
        [
            pltpu.SMEM(rows.shape, rows.dtype),
            pltpu.SMEM(cols.shape, cols.dtype),
            pltpu.SMEM(live.shape, live.dtype),
            pltpu.VMEM(vectors.shape, f32),
            pltpu.VMEM(damage.shape, f32),
            pltpu.VMEM((vecs, here * size), bf16),
            pltpu.VMEM(upper.shape, bf16),
            pltpu.VMEM((REACH * here + 1, vecs, size), f32),
            pltpu.VMEM((here + 1, 2 * vecs, size), bf16),
            pltpu.VMEM((here + 1, 2 * vecs, size), bf16),
            pltpu.SemaphoreType.DMA((len(PIECES),)),
            pltpu.SemaphoreType.DMA((5,)),
            pltpu.SemaphoreType.DMA((groups,)),
        ],
        BLOCKS_STAY, 2 * slots * vecs * size * size, 2 * slots * size * size,
    )(in_hbm(rows), in_hbm(cols), live, in_hbm(vectors), in_hbm(damage), in_hbm(upper))


def forward(
    owners, rows, cols, live, blocks, far, back, swap, mate, own, diag, every, damage, upper
):
    f32, bf16 = jnp.float32, jnp.bfloat16
    here, vecs, size = blocks.shape
    slots = upper.shape[0]
    return call(
        forward_kernel, "forward", [SM] * 3 + [VM] * 9 + [FAR],
        [((vecs, here * size), f32), ((owners, vecs // 2, 2 * every.shape[0]), bf16)],
        [
            pltpu.VMEM((vecs, here * size), f32),
            pltpu.VMEM(upper.shape, bf16),
            pltpu.VMEM((here + 1, vecs, size), f32),
            pltpu.VMEM((REACH * here + 1, 2 * vecs, size), bf16),
            pltpu.VMEM((REACH * here + 1, 2 * vecs, size), bf16),
            pltpu.SemaphoreType.DMA((len(LATE_PIECES),)),
            pltpu.SemaphoreType.DMA(()),
        ],
        BLOCKS_STAY, 2 * slots * vecs * size * size, 2 * slots * size * size,
    )(rows, cols, live, blocks, far, back, swap, mate, own, diag, every, damage, in_hbm(upper))


def on_device(vectors, damage, diag_blocks, upper_blocks, block_rows, block_cols, live_slots):
    f32, bf16 = jnp.float32, jnp.bfloat16
    vecs, width = vectors.shape
    here, size = diag_blocks.shape[:2]
    owners, groups = lax.axis_size("rows"), lax.axis_size("vec")
    damage = damage.reshape(here, size)
    rim = (RIM, vecs, size)

    copies, blocks, edge, own, one, chips, swap = backward(
        groups, block_rows, block_cols, live_slots, vectors, damage, upper_blocks
    )
    every = lax.all_to_all(copies, "vec", 0, 0).reshape(groups * vecs, width)

    down = [(d, d - 2) for d in range(2, owners)]
    up = [(d, d + 2) for d in range(owners - 2)]
    across = [(d, d + 3) for d in range(1, owners - 3, 2)]
    across += [(b, a) for a, b in across]
    mates = [(d, d ^ 1) for d in range(owners)]

    far = lax.ppermute(edge, "rows", down)
    chips = lax.ppermute(chips, "rows", up)
    swap = lax.ppermute(swap, "rows", across)
    mate, back = call(
        relay_kernel, "relay", [VM] * 5, [((3,) + rim, f32), (rim, f32)], [], SMALL_VMEM,
        0, 8 * size,
    )(edge, far, one, chips, swap)
    mate = lax.ppermute(mate, "rows", mates)

    product, partials = forward(
        owners, block_rows, block_cols, live_slots, blocks, far, back, swap, mate, own, diag_blocks,
        every, damage, upper_blocks,
    )
    partials = lax.all_to_all(partials, "rows", 0, 0)
    (projected,) = call(
        functools.partial(sum_kernel, 1.0 / (width * owners)), "sum", [VM],
        [((vecs, groups * vecs), f32)], [], SMALL_VMEM, 0, partials.size * 2,
    )(partials)
    return (product, projected)


def solution(mesh):
    return jax.shard_map(
        on_device,
        mesh=mesh,
        in_specs=(
            P("vec", "rows"),
            P("rows"),
            P("rows", None, None),
            P("rows", None, None),
            P("rows"),
            P("rows"),
            P("rows"),
        ),
        out_specs=(P("vec", "rows"), P("vec", None)),
        check_vma=False,
    )
```

```python
import functools

import jax
import jax.numpy as jnp
from jax import lax
from jax.experimental import pallas as pl
from jax.experimental.pallas import tpu as pltpu
from jax.sharding import PartitionSpec as P

REACH = 4
RIM = 6
PIECES = (32, 32, 32, 32)
LATE_PIECES = (64, 64)
SMALL_VMEM = 8 << 20
BLOCKS_STAY = 16 << 20


resid_eta = 0.001

VM = pl.BlockSpec(memory_space=pltpu.VMEM)
SM = pl.BlockSpec(memory_space=pltpu.SMEM)
FAR = pl.BlockSpec(memory_space=pl.ANY)
TRANSPOSED = (((1,), (1,)), ((), ()))


def in_hbm(array):
    return pltpu.with_memory_space_constraint(array, pltpu.HBM)


def call(kernel, name, in_specs, outs, scratch, vmem, flops, moved):
    return pl.pallas_call(
        kernel,
        name=name,
        in_specs=in_specs,
        out_specs=[FAR if i == 0 else VM for i in range(len(outs))] if scratch else [VM] * len(outs),
        out_shape=[jax.ShapeDtypeStruct(shape, dtype) for shape, dtype in outs],
        scratch_shapes=scratch,
        compiler_params=pltpu.CompilerParams(vmem_limit_bytes=vmem),
        cost_estimate=pl.CostEstimate(flops=flops, bytes_accessed=moved, transcendentals=0),
    )


def softness(damage):
    return jnp.sqrt((1.0 - damage) ** 2 + resid_eta)


def put_halves(top, bottom, at, x):
    z = jnp.zeros_like(x)
    top[at] = jnp.concatenate([x, z], 0).astype(jnp.bfloat16)
    bottom[at] = jnp.concatenate([z, x], 0).astype(jnp.bfloat16)


def streamed(upper_far, upper, sems, pieces):
    copies, first = [], 0
    for i, count in enumerate(pieces):
        cut = pl.ds(first, count)
        copies.append(pltpu.make_async_copy(upper_far.at[cut], upper.at[cut], sems.at[i]))
        first += count
    assert first == upper.shape[0]
    return copies


def each_pair(first, count, live, take, give, top, bottom, total, product):
    vecs = total.shape[1]
    none_from, none_to = top.shape[0] - 1, total.shape[0] - 1

    def taken(s):
        return jnp.where(s < live, take(s), none_from)

    results = []
    for s in range(first, first + count, 2):
        y = product(jnp.concatenate([top[taken(s)], bottom[taken(s + 1)]], axis=1), s)
        results += [y[:vecs], y[vecs:]]
    for k in range(count):
        s = first + k
        total[jnp.where(s < live, give(s), none_to)] += results[k]


def backward_kernel(
    rows_far, cols_far, live_far, vectors_far, damage_far, upper_far, everyones_far, blocks, rim,
    own, one, chips, swap, rows, cols, live, vectors, damage, flat, upper, total, top, bottom, sems,
    few_sems, out_sems
):
    here = own.shape[0]
    size = upper.shape[1]
    few = [
        pltpu.make_async_copy(source, target, few_sems.at[i])
        for i, (source, target) in enumerate(
            ((vectors_far, vectors), (damage_far, damage), (rows_far, rows), (cols_far, cols),
             (live_far, live))
        )
    ]
    copies = streamed(upper_far, upper, sems, PIECES)
    for copy in few + copies:
        copy.start()
    mine = lax.axis_index("rows")
    total[...] = jnp.zeros_like(total)
    for copy in few:
        copy.wait()
    soft = softness(damage[...])
    for b in range(here):
        cut = slice(b * size, (b + 1) * size)
        scaled = (vectors[:, cut] * soft[b : b + 1, :]).astype(jnp.bfloat16)
        blocks[b] = scaled
        if b < RIM:
            rim[b] = scaled.astype(jnp.float32)
        flat[:, cut] = scaled
        put_halves(top, bottom, b, scaled.astype(jnp.float32))
    put_halves(top, bottom, here, jnp.zeros(total.shape[1:], jnp.float32))
    rim[RIM:] = jnp.zeros((rim.shape[0] - RIM,) + rim.shape[1:], jnp.float32)
    gifts = [
        pltpu.make_async_copy(flat, everyones_far.at[i], out_sems.at[i])
        for i in range(everyones_far.shape[0])
    ]
    for gift in gifts:
        gift.start()

    def product(x, s):
        pair = upper[pl.ds(s, 2)].reshape(2 * size, size)
        return jnp.dot(x, pair, preferred_element_type=jnp.float32)

    first = 0
    for copy, count in zip(copies, PIECES):
        copy.wait()
        each_pair(
            first, count, live[0], lambda s: rows[s] - mine * here, lambda s: cols[s] - mine * here,
            top, bottom, total, product,
        )
        first += count
    own[...] = total[:here]
    one[...] = total[here : here + RIM]
    second_core = lax.rem(mine, 2)
    other = jnp.where(second_core == 1, here, 3 * here)
    chips[0] = total[2 * here : 2 * here + RIM]
    chips[1] = total[pl.ds(other, RIM)]
    swap[...] = jnp.where(
        second_core == 1, total[3 * here : 3 * here + RIM], blocks[:RIM].astype(jnp.float32)
    )
    for gift in gifts:
        gift.wait()


def relay_kernel(rim, far, one, chips, swap, out, back):
    first_core = lax.rem(lax.axis_index("rows"), 2) == 0
    out[0] = rim[:RIM]
    out[1] = far[:RIM]
    out[2] = chips[1] + jnp.where(first_core, one[...], 0.0)
    back[...] = chips[0] + jnp.where(first_core, swap[...], 0.0)


def forward_kernel(
    rows, cols, live, blocks, far, back, swap, mate, own, diag, every, damage, upper_far,
    product_far, copies_out, product_near, upper, total, top, bottom, sems, out_sem
):
    here = own.shape[0]
    size = diag.shape[1]
    vecs = blocks.shape[1]
    copies = streamed(upper_far, upper, sems, LATE_PIECES)
    for copy in copies:
        copy.start()
    mine = lax.axis_index("rows")
    second_core = lax.rem(mine, 2) == 1
    for b in range(here):
        put_halves(top, bottom, b, blocks[b].astype(jnp.float32))
    for b in range(RIM):
        put_halves(top, bottom, here + b, jnp.where(second_core, mate[1, b], mate[0, b]))
        put_halves(top, bottom, 2 * here + b, far[b].astype(jnp.float32))
        put_halves(top, bottom, 3 * here + b, jnp.where(second_core, swap[b], mate[1, b]))
    put_halves(top, bottom, REACH * here, jnp.zeros((vecs, size), jnp.float32))
    for b in range(here):
        total[b] = own[b] + lax.dot_general(
            blocks[b], diag[b], TRANSPOSED, preferred_element_type=jnp.float32
        )
    total[:RIM] += back[...] + mate[2]

    def product(x, s):
        pair = jnp.concatenate([upper[s], upper[s + 1]], axis=1)
        return lax.dot_general(x, pair, TRANSPOSED, preferred_element_type=jnp.float32)

    first = 0
    for copy, count in zip(copies, LATE_PIECES):
        copy.wait()
        each_pair(
            first, count, live[0], lambda s: cols[s] - mine * here, lambda s: rows[s] - mine * here,
            top, bottom, total, product,
        )
        first += count
    soft = softness(damage[...])
    for b in range(here):
        product_near[:, b * size : (b + 1) * size] = total[b] * soft[b : b + 1, :]
    leave = pltpu.make_async_copy(product_near, product_far, out_sem)
    leave.start()
    gram = jnp.zeros((2 * vecs, every.shape[0]), jnp.float32)
    for b in range(here):
        raw = total[b]
        high = raw.astype(jnp.bfloat16)
        low = (raw - high.astype(jnp.float32)).astype(jnp.bfloat16)
        gram += lax.dot_general(
            jnp.concatenate([high, low], 0), every[:, b * size : (b + 1) * size], TRANSPOSED,
            preferred_element_type=jnp.float32,
        )
    gram = gram[:vecs] + gram[vecs:]
    half = vecs // 2
    packed = jnp.concatenate([gram[:half], gram[half:]], axis=1)
    copies_out[...] = jnp.broadcast_to(packed[None], copies_out.shape)
    leave.wait()


def sum_kernel(scale, parts, out):
    packed = jnp.sum(parts[...], axis=0) * scale
    columns = out.shape[1]
    half = packed.shape[0]
    out[:half] = packed[:, :columns]
    out[half:] = packed[:, columns:]


def backward(groups, rows, cols, live, vectors, damage, upper):
    f32, bf16 = jnp.float32, jnp.bfloat16
    vecs = vectors.shape[0]
    here, size = damage.shape
    slots = upper.shape[0]
    rim = (RIM, vecs, size)
    return call(
        backward_kernel, "backward", [FAR] * 6,
        [
            ((groups, vecs, here * size), bf16), ((here, vecs, size), bf16), ((RIM + 1, vecs, size), f32),
            ((here, vecs, size), f32), (rim, f32), ((2,) + rim, f32), (rim, f32),
        ],
        [
            pltpu.SMEM(rows.shape, rows.dtype),
            pltpu.SMEM(cols.shape, cols.dtype),
            pltpu.SMEM(live.shape, live.dtype),
            pltpu.VMEM(vectors.shape, f32),
            pltpu.VMEM(damage.shape, f32),
            pltpu.VMEM((vecs, here * size), bf16),
            pltpu.VMEM(upper.shape, bf16),
            pltpu.VMEM((REACH * here + 1, vecs, size), f32),
            pltpu.VMEM((here + 1, 2 * vecs, size), bf16),
            pltpu.VMEM((here + 1, 2 * vecs, size), bf16),
            pltpu.SemaphoreType.DMA((len(PIECES),)),
            pltpu.SemaphoreType.DMA((5,)),
            pltpu.SemaphoreType.DMA((groups,)),
        ],
        BLOCKS_STAY, 2 * slots * vecs * size * size, 2 * slots * size * size,
    )(in_hbm(rows), in_hbm(cols), live, in_hbm(vectors), in_hbm(damage), in_hbm(upper))


def forward(
    owners, rows, cols, live, blocks, far, back, swap, mate, own, diag, every, damage, upper
):
    f32, bf16 = jnp.float32, jnp.bfloat16
    here, vecs, size = blocks.shape
    slots = upper.shape[0]
    return call(
        forward_kernel, "forward", [SM] * 3 + [VM] * 9 + [FAR],
        [((vecs, here * size), f32), ((owners, vecs // 2, 2 * every.shape[0]), f32)],
        [
            pltpu.VMEM((vecs, here * size), f32),
            pltpu.VMEM(upper.shape, bf16),
            pltpu.VMEM((here + 1, vecs, size), f32),
            pltpu.VMEM((REACH * here + 1, 2 * vecs, size), bf16),
            pltpu.VMEM((REACH * here + 1, 2 * vecs, size), bf16),
            pltpu.SemaphoreType.DMA((len(LATE_PIECES),)),
            pltpu.SemaphoreType.DMA(()),
        ],
        BLOCKS_STAY, 2 * slots * vecs * size * size, 2 * slots * size * size,
    )(rows, cols, live, blocks, far, back, swap, mate, own, diag, every, damage, in_hbm(upper))


def on_device(vectors, damage, diag_blocks, upper_blocks, block_rows, block_cols, live_slots):
    f32, bf16 = jnp.float32, jnp.bfloat16
    vecs, width = vectors.shape
    here, size = diag_blocks.shape[:2]
    owners, groups = lax.axis_size("rows"), lax.axis_size("vec")
    damage = damage.reshape(here, size)
    rim = (RIM, vecs, size)

    copies, blocks, edge, own, one, chips, swap = backward(
        groups, block_rows, block_cols, live_slots, vectors, damage, upper_blocks
    )
    every = lax.all_to_all(copies, "vec", 0, 0).reshape(groups * vecs, width)

    down = [(d, d - 2) for d in range(2, owners)]
    up = [(d, d + 2) for d in range(owners - 2)]
    across = [(d, d + 3) for d in range(1, owners - 3, 2)]
    across += [(b, a) for a, b in across]
    mates = [(d, d ^ 1) for d in range(owners)]

    far = lax.ppermute(edge, "rows", down)
    chips = lax.ppermute(chips, "rows", up)
    swap = lax.ppermute(swap, "rows", across)
    mate, back = call(
        relay_kernel, "relay", [VM] * 5, [((3,) + rim, f32), (rim, f32)], [], SMALL_VMEM,
        0, 8 * size,
    )(edge, far, one, chips, swap)
    mate = lax.ppermute(mate, "rows", mates)

    product, partials = forward(
        owners, block_rows, block_cols, live_slots, blocks, far, back, swap, mate, own, diag_blocks,
        every, damage, upper_blocks,
    )
    partials = lax.all_to_all(partials, "rows", 0, 0)
    (projected,) = call(
        functools.partial(sum_kernel, 1.0 / (width * owners)), "sum", [VM],
        [((vecs, groups * vecs), f32)], [], SMALL_VMEM, 0, partials.size * 4,
    )(partials)
    return (product, projected)


def solution(mesh):
    return jax.shard_map(
        on_device,
        mesh=mesh,
        in_specs=(
            P("vec", "rows"),
            P("rows"),
            P("rows", None, None),
            P("rows", None, None),
            P("rows"),
            P("rows"),
            P("rows"),
        ),
        out_specs=(P("vec", "rows"), P("vec", None)),
        check_vma=False,
    )
```
